32 devices in a mesh: rows: 16 (over z, y, core), seq: 2 (over x).
Axes of the slice: x: 2, y: 2, z: 4, core: 2. Of those that a mesh axis runs over, the one named last changes fastest.
Arguments:
- layer_input: bfloat16 [16, 1664, 768], P('rows', 'seq'), may hold values from -6 to 6
- out_cotangent: bfloat16 [16, 1664, 768], P('rows', 'seq'), may hold values from -6 to 6
- gain1: float32 [768], replicated, may hold values from 0.5 to 1.5
- shift1: float32 [768], replicated, may hold values from -1.5 to 1.5
- w_qkv: bfloat16 [768, 2304], replicated, may hold values from -0.21875 to 0.21875
- bias_q: float32 [768], replicated, may hold values from -1.5 to 1.5
- bias_v: float32 [768], replicated, may hold values from -1.5 to 1.5
- w_out: bfloat16 [768, 768], replicated, may hold values from -2.5 to 2.5
- bias_out: float32 [768], replicated, may hold values from -1.5 to 1.5
- gain2: float32 [768], replicated, may hold values from 0.5 to 1.5
- shift2: float32 [768], replicated, may hold values from -1.5 to 1.5
- w_up: bfloat16 [768, 3072], replicated, may hold values from -0.21875 to 0.21875
- bias_up: float32 [3072], replicated, may hold values from -1.5 to 1.5
- w_down: bfloat16 [3072, 768], replicated, may hold values from -0.109375 to 0.109375
- bias_down: float32 [768], replicated, may hold values from -1.5 to 1.5
- segment_ids: int32 [16, 1664], P('rows'), may hold values from 0 to 12, never falling along the last dimension, each value on 1 to 832 neighbouring positions
- valid_mask: int32 [16, 1664], P('rows'), may hold values from 0 to 1, as said below
Outputs:
- layer_output: float32 [16, 1664, 768], P('rows', 'seq')
- grad_x: float32 [16, 1664, 768], P('rows', 'seq')
- grad_gain1: float32 [768], P(('rows', 'seq'))
- grad_shift1: float32 [768], P(('rows', 'seq'))
- grad_w_qkv: float32 [768, 2304], P(('rows', 'seq'))
- grad_bias_q: float32 [768], P(('rows', 'seq'))
- grad_bias_v: float32 [768], P(('rows', 'seq'))
- grad_w_out: float32 [768, 768], P(('rows', 'seq'))
- grad_bias_out: float32 [768], P(('rows', 'seq'))
- grad_gain2: float32 [768], P(('rows', 'seq'))
- grad_shift2: float32 [768], P(('rows', 'seq'))
- grad_w_up: float32 [768, 3072], P(('rows', 'seq'))
- grad_bias_up: float32 [3072], P(('rows', 'seq'))
- grad_w_down: float32 [3072, 768], P(('rows', 'seq'))
- grad_bias_down: float32 [768], P(('rows', 'seq'))
The draws below stay inside these ranges and needn't reach their ends.
Inputs may be any that keep to these rules, and one draw needn't show every extreme that they name: `segment_ids`: within a row the segment numbers never fall; one segment is one image's tokens. `valid_mask`: in each row the tokens marked 1 come first, and the row ends in at least one token marked 0.
All inputs are finite; a program needn't handle non-finite values.
Results may differ from the reference program's by a relative error of at most 0.011.
Values may be sent and summed in bfloat16 or wider, within the bound.
No kernel may reach another device: no remote copies, remote signals or barrier semaphores. Data moves between devices by JAX's collectives and lax.ppermute only.
A program may use at most 192 MiB of HBM per device.

```python
import math
import jax
import jax.numpy as jnp
import numpy as np
from jax import lax

D = 768
HEADS = 12
HEAD_DIM = 64
FF = 3072
L = 1664
ROWS = 16


def draw_valid_mask(key, part):
    padding = jax.random.randint(key, (ROWS, 1), 1, L // 8 + 1)
    positions = jnp.arange(L)[None, :]
    return (positions < L - padding).astype(jnp.int32)


def strengthened(entries, own_key, source, target, shards_of, factor):
    def block_of(dim):
        return (jnp.arange(entries.shape[dim]) // (entries.shape[dim] // shards_of)).reshape((-1,) + (1,) * (entries.ndim - 1 - dim))

    near = jax.random.permutation(own_key, shards_of)[block_of(target)]
    far = (block_of(target) + shards_of // 2) % shards_of
    return jnp.where((block_of(source) == near) | (block_of(source) == far), factor * entries, entries)


def block_scale(rng, dims, split, smallest, top_value):
    level = 1.0
    for position, parts in split:
        draws = jax.random.uniform(jax.random.fold_in(jax.random.fold_in(rng, 6), position), (parts,), jnp.float32, smallest / len(split), top_value / len(split))
        level = level * jnp.repeat(jnp.exp(draws), dims[position] // parts).reshape((-1,) + (1,) * (len(dims) - 1 - position))
    return level


def profile(amount, total, most, lean):
    loads = [(1 << 20) // math.isqrt(standing ** lean) + 1 for standing in range(2, amount + 1)]
    rest, holding = total - most - (amount - 1), [1] * (amount - 1)
    while rest > 0:
        movable = [i for i in range(amount - 1) if holding[i] < most]
        pool, left = sum([loads[i] for i in movable]), rest
        for i in movable:
            addition = min(most - holding[i], max(1, left * loads[i] // pool), rest)
            holding[i] = holding[i] + addition
            rest = rest - addition
    return np.array([most] + holding)


def uneven_parts(rng, number_of, total, reach, slope):
    if number_of == 2:
        one = jax.random.randint(rng, (), max(1, total - reach), min(reach, total - 1) + 1)
        return jnp.stack([one, total - one])
    lengths = jnp.asarray(profile(number_of, total, reach, slope), jnp.int32)
    pairs = (number_of - 1) // 2
    giver, sink = lengths[1:1 + 2 * pairs:2], lengths[2:2 + 2 * pairs:2]
    slack = jnp.minimum(giver - 1, reach - sink)
    shifted = jax.random.randint(jax.random.fold_in(rng, 1), (pairs,), 0, 1 << 20) % (slack + 1)
    lengths = lengths.at[1:1 + 2 * pairs:2].set(giver - shifted).at[2:2 + 2 * pairs:2].set(sink + shifted)
    return lengths[jax.random.permutation(jax.random.fold_in(rng, 2), number_of)]


def bell_draw(rng, dims, width, bound, shards=(), dtype=jnp.bfloat16):
    loudness = block_scale(rng, dims, shards, -0.22, 0.18) if shards else 1.0
    result = jax.random.normal(rng, dims, jnp.float32) * width * loudness
    return jnp.minimum(jnp.maximum(result, -bound), bound).astype(dtype)


def heavy_noise(own_key, shape, width, limit, cuts, heavy, dtype=jnp.bfloat16):
    values = width * jax.random.normal(own_key, shape, jnp.float32)
    if cuts:
        values = values * block_scale(own_key, shape, cuts, -0.22, 0.18)
    return jnp.clip(strengthened(values, jax.random.fold_in(own_key, 3), *heavy), -limit, limit).astype(dtype)


def setup_inputs(seed: int = 0) -> dict:
    key_list = jax.random.split(jax.random.key(seed), 18)
    layer_input = bell_draw(key_list[0], (ROWS, L, D), 1.0, 6.0, ((0, 16), (1, 2)))
    out_cotangent = heavy_noise(key_list[1], (ROWS, L, D), 1.0, 6.0, ((0, 16), (1, 2)), (0, 2, 16, 2.0))
    gain1 = jnp.clip(1.0 + 0.1 * jax.random.normal(key_list[2], (D,), jnp.float32), 0.5, 1.5)
    shift1 = bell_draw(key_list[3], (D,), 0.3, 1.5, (), jnp.float32)
    w_qkv = bell_draw(key_list[4], (D, 3 * D), D ** -0.5, 0.21875)
    bias_q = bell_draw(key_list[5], (D,), 0.3, 1.5, (), jnp.float32)
    bias_v = bell_draw(key_list[6], (D,), 0.3, 1.5, (), jnp.float32)
    w_out = bell_draw(key_list[7], (D, D), (max(1, D * max(3, L // 128) // L)) ** -0.5, 2.5)
    bias_out = bell_draw(key_list[8], (D,), 0.3, 1.5, (), jnp.float32)
    gain2 = jnp.clip(1.0 + 0.1 * jax.random.normal(key_list[9], (D,), jnp.float32), 0.5, 1.5)
    shift2 = bell_draw(key_list[10], (D,), 0.3, 1.5, (), jnp.float32)
    w_up = bell_draw(key_list[11], (D, FF), D ** -0.5, 0.21875)
    bias_up = bell_draw(key_list[12], (FF,), 0.3, 1.5, (), jnp.float32)
    w_down = bell_draw(key_list[13], (FF, D), FF ** -0.5, 0.109375)
    bias_down = bell_draw(key_list[14], (D,), 0.3, 1.5, (), jnp.float32)
    segment_ids = jax.vmap(lambda own: jnp.searchsorted(jnp.cumsum(uneven_parts(own, max(3, L // 128), L, L // 2, 1)), jnp.arange(L), side="right"))(jax.random.split(key_list[15], ROWS)).reshape((ROWS, L)).astype(jnp.int32)
    valid_mask = draw_valid_mask(jax.random.fold_in(key_list[17], 71), 0)
    return {"layer_input": layer_input, "out_cotangent": out_cotangent, "gain1": gain1, "shift1": shift1, "w_qkv": w_qkv, "bias_q": bias_q, "bias_v": bias_v, "w_out": w_out, "bias_out": bias_out, "gain2": gain2, "shift2": shift2, "w_up": w_up, "bias_up": bias_up, "w_down": w_down, "bias_down": bias_down, "segment_ids": segment_ids, "valid_mask": valid_mask}


@jax.custom_vjp
def low(v):
    return lax.optimization_barrier(v.astype(jnp.bfloat16)).astype(jnp.float32)

@jax.custom_vjp
def low_back(v):
    return v

def low_keep(v):
    return (low(v), None)

def low_pass(kept, grad):
    return (grad,)

def back_keep(v):
    return (v, None)

def back_low(kept, grad):
    return (low(grad),)
low.defvjp(low_keep, low_pass)
low_back.defvjp(back_keep, back_low)

def matmul(left, right):
    return jnp.dot(left, right, precision=lax.Precision.HIGHEST, preferred_element_type=jnp.float32)

def layer_norm(values, gain, shift):
    center = lax.optimization_barrier(jnp.mean(values, axis=-1, keepdims=True))
    centered = values - center
    spread = lax.optimization_barrier(jnp.mean(centered * centered, axis=-1, keepdims=True))
    return centered * lax.rsqrt(spread + 1e-06) * gain + shift

def row_attention(item):
    queries, keys_row, values_row, seg_row, valid_row = item
    scale = HEAD_DIM ** (-0.5)
    scores = jnp.einsum('qhd,khd->hqk', queries, keys_row, precision=lax.Precision.HIGHEST) * scale
    scores = low_back(scores)
    index_row = jnp.arange(L)
    allowed = (seg_row[:, None] == seg_row[None, :]) & (valid_row[None, :] == 1) | (index_row[:, None] == index_row[None, :])
    scores = jnp.where(allowed[None], scores, -1e+30)
    probs = jax.nn.softmax(scores, axis=-1)
    context = jnp.einsum('hqk,khd->qhd', low(probs), values_row, precision=lax.Precision.HIGHEST)
    return context.reshape(L, D)

def forward(inputs, params, seg_group, valid_group):
    gain1, shift1, w_qkv, bias_q, bias_v, w_out, bias_out, gain2, shift2, w_up, bias_up, w_down, bias_down = params
    group_rows = inputs.shape[0]
    flat = inputs.reshape(group_rows * L, D)
    normed1 = low(layer_norm(flat, gain1, shift1))
    bias_all = jnp.concatenate([bias_q, jnp.zeros_like(bias_q), bias_v])
    qkv = low(low_back(matmul(normed1, w_qkv) + bias_all))
    qkv = qkv.reshape(group_rows, L, 3, HEADS, HEAD_DIM)
    context = lax.map(jax.checkpoint(row_attention), (qkv[:, :, 0], qkv[:, :, 1], qkv[:, :, 2], seg_group, valid_group))
    context = low(low_back(context)).reshape(group_rows * L, D)
    attn = low_back(matmul(context, w_out) + bias_out)
    hidden = flat + attn
    normed2 = low(layer_norm(hidden, gain2, shift2))
    upper = low_back(matmul(normed2, w_up) + bias_up)
    act = low(jax.nn.gelu(upper, approximate=False))
    ffn = low_back(matmul(act, w_down) + bias_down)
    return (hidden + ffn).reshape(group_rows, L, D)

def reference(layer_input, out_cotangent, gain1, shift1, w_qkv, bias_q, bias_v, w_out, bias_out, gain2, shift2, w_up, bias_up, w_down, bias_down, segment_ids, valid_mask):
    params = (gain1.astype(jnp.float32), shift1.astype(jnp.float32), w_qkv.astype(jnp.float32), bias_q.astype(jnp.float32), bias_v.astype(jnp.float32), w_out.astype(jnp.float32), bias_out.astype(jnp.float32), gain2.astype(jnp.float32), shift2.astype(jnp.float32), w_up.astype(jnp.float32), bias_up.astype(jnp.float32), w_down.astype(jnp.float32), bias_down.astype(jnp.float32))
    group = 2 if ROWS % 2 == 0 else 1
    count = ROWS // group
    inputs = layer_input.astype(jnp.float32).reshape(count, group, L, D)
    cotangent = out_cotangent.astype(jnp.float32).reshape(count, group, L, D)
    seg_all = segment_ids.reshape(count, group, L)
    valid_all = valid_mask.reshape(count, group, L)

    def step(carry, item):
        x_group, cot_group, seg_group, valid_group = item

        def apply(x_val, param_val):
            return forward(x_val, param_val, seg_group, valid_group)
        output, pullback = jax.vjp(apply, x_group, params)
        grad_group, grad_params = pullback(cot_group)
        carry = jax.tree.map(lambda left, right: left + right, carry, grad_params)
        return (carry, (output, grad_group))
    zeros = tuple((jnp.zeros_like(member) for member in params))
    totals, (outputs, grads) = lax.scan(step, zeros, (inputs, cotangent, seg_all, valid_all))
    return (outputs.reshape(ROWS, L, D), grads.reshape(ROWS, L, D), totals[0], totals[1], totals[2], totals[3], totals[4], totals[5], totals[6], totals[7], totals[8], totals[9], totals[10], totals[11], totals[12])
```

```python
import jax
import jax.numpy as jnp
from jax import lax
from jax.experimental import pallas as pl
from jax.experimental.pallas import tpu as pltpu
from jax.sharding import PartitionSpec as P

HEADS = 12
HEAD_DIM = 64
BQ = 128
BK = 256
PAIR = 2 * HEAD_DIM
LOG2E = 1.4426950408889634
NEG = -1e30

f32 = jnp.float32
bf16 = jnp.bfloat16


def left_dot(left, right):
    return lax.dot_general(left, right, (((0,), (0,)), ((), ())), preferred_element_type=f32)


def right_dot(left, right):
    return lax.dot_general(left, right, (((1,), (1,)), ((), ())), preferred_element_type=f32)


def mm(left, right):
    return jnp.dot(left, right, preferred_element_type=f32)


def stack_heads(block):
    lane = lax.broadcasted_iota(jnp.int32, block.shape, 1)
    zero = jnp.zeros_like(block)
    return jnp.concatenate(
        [jnp.where(lane < HEAD_DIM, block, zero), jnp.where(lane < HEAD_DIM, zero, block)], axis=0
    )


def block_bias(kseg_ref, qseg_ref, qs, ks):
    same = kseg_ref[pl.ds(ks, BK), :] == qseg_ref[0:1, pl.ds(qs, BQ)]
    row = lax.broadcasted_iota(jnp.int32, (BK, BQ), 0)
    col = lax.broadcasted_iota(jnp.int32, (BK, BQ), 1)
    same = same | ((row - col) == (qs - ks))
    bias = jnp.where(same, 0.0, NEG)
    return jnp.concatenate([bias, bias], axis=1)


def forward_kernel(start_ref, count_ref, qkv_ref, kseg_ref, qseg_ref, ctx_ref, lse_ref, kpad, vt, qst, acc):
    full, cols = qkv_ref.shape
    width = cols // 3
    pairs = width // PAIR
    kpad[0:full, :] = qkv_ref[:, width : 2 * width]
    kpad[full:, :] = jnp.zeros((kpad.shape[0] - full, width), bf16)
    vt[:, full:] = jnp.zeros((width, vt.shape[1] - full), bf16)
    for i in range(full // BQ):
        for p in range(pairs):
            blk = qkv_ref[i * BQ : (i + 1) * BQ, 2 * width + p * PAIR : 2 * width + (p + 1) * PAIR]
            vt[p * PAIR : (p + 1) * PAIR, i * BQ : (i + 1) * BQ] = blk.T

    def q_step(i, _):
        qs = pl.multiple_of(i * BQ, BQ)
        start = start_ref[i]
        for p in range(pairs):
            blk = qkv_ref[pl.ds(qs, BQ), p * PAIR : (p + 1) * PAIR]
            qst[p] = stack_heads(blk * jnp.asarray(HEAD_DIM**-0.5, bf16))
            acc[p] = jnp.zeros((PAIR, BQ), f32)

        def k_step(t, carry):
            ks = pl.multiple_of(start + t * BK, BQ)
            bias = block_bias(kseg_ref, qseg_ref, qs, ks)
            new = []
            for p in range(pairs):
                top, total = carry[p]
                s = right_dot(kpad[pl.ds(ks, BK), p * PAIR : (p + 1) * PAIR], qst[p])
                s = s * LOG2E + bias
                top_new = jnp.maximum(top, jnp.max(s, axis=0, keepdims=True))
                e = jnp.exp2(s - top_new)
                alpha = jnp.exp2(top - top_new)
                total = total * alpha + jnp.sum(e, axis=0, keepdims=True)
                e = e.astype(bf16)
                for h in range(2):
                    rows = slice(h * HEAD_DIM, (h + 1) * HEAD_DIM)
                    lanes = slice(h * BQ, (h + 1) * BQ)
                    part = mm(vt[p * PAIR + h * HEAD_DIM : p * PAIR + (h + 1) * HEAD_DIM, pl.ds(ks, BK)], e[:, lanes])
                    acc[p, rows, :] = acc[p, rows, :] * alpha[:, lanes] + part
                new.append((top_new, total))
            return tuple(new)

        init = tuple((jnp.full((1, 2 * BQ), NEG, f32), jnp.zeros((1, 2 * BQ), f32)) for _ in range(pairs))
        done = lax.fori_loop(0, count_ref[i], k_step, init)
        for p in range(pairs):
            top, total = done[p]
            inv = 1.0 / total
            half = []
            for h in range(2):
                half.append(acc[p, h * HEAD_DIM : (h + 1) * HEAD_DIM, :] * inv[:, h * BQ : (h + 1) * BQ])
            ctx_ref[pl.ds(qs, BQ), p * PAIR : (p + 1) * PAIR] = jnp.concatenate(half, axis=0).T.astype(bf16)
            lse = top + jnp.log2(total)
            lse_ref[p, pl.ds(i, 1), :] = lse
        return 0

    lax.fori_loop(0, full // BQ, q_step, 0)


def backward_kernel(
    start_ref, count_ref, qkv_ref, kseg_ref, qseg_ref, ctx_ref, lse_ref, dctx_ref, out_ref, kpad, vpad, kt, qst, dst, acc, dk, dv
):
    full, cols = qkv_ref.shape
    width = cols // 3
    pairs = width // PAIR
    pad = kpad.shape[0] - full
    kpad[0:full, :] = qkv_ref[:, width : 2 * width]
    kpad[full:, :] = jnp.zeros((pad, width), bf16)
    vpad[0:full, :] = qkv_ref[:, 2 * width :]
    vpad[full:, :] = jnp.zeros((pad, width), bf16)
    kt[:, full:] = jnp.zeros((width, pad), bf16)
    dk[...] = jnp.zeros(dk.shape, f32)
    dv[...] = jnp.zeros(dv.shape, f32)
    for i in range(full // BQ):
        for p in range(pairs):
            blk = qkv_ref[i * BQ : (i + 1) * BQ, width + p * PAIR : width + (p + 1) * PAIR]
            kt[p * PAIR : (p + 1) * PAIR, i * BQ : (i + 1) * BQ] = blk.T
    head_row = lax.broadcasted_iota(jnp.int32, (8, PAIR), 0)
    head_lane = lax.broadcasted_iota(jnp.int32, (8, PAIR), 1) // HEAD_DIM
    pick = (head_row == head_lane).astype(f32)

    def q_step(i, _):
        qs = pl.multiple_of(i * BQ, BQ)
        start = start_ref[i]
        stats = []
        for p in range(pairs):
            lanes = slice(p * PAIR, (p + 1) * PAIR)
            blk = qkv_ref[pl.ds(qs, BQ), lanes]
            qst[p] = stack_heads(blk * jnp.asarray(HEAD_DIM**-0.5, bf16))
            grad = dctx_ref[pl.ds(qs, BQ), lanes]
            dst[p] = stack_heads(grad)
            acc[p] = jnp.zeros((PAIR, BQ), f32)
            prod = grad.astype(f32) * ctx_ref[pl.ds(qs, BQ), lanes].astype(f32)
            dots = lax.dot_general(
                pick, prod, (((1,), (1,)), ((), ())), precision=lax.Precision.HIGHEST, preferred_element_type=f32
            )
            stats.append((lse_ref[p, pl.ds(i, 1), :], jnp.concatenate([dots[0:1], dots[1:2]], axis=1)))

        def k_step(t, _):
            ks = pl.multiple_of(start + t * BK, BQ)
            bias = block_bias(kseg_ref, qseg_ref, qs, ks)
            for p in range(pairs):
                lanes = slice(p * PAIR, (p + 1) * PAIR)
                lse, dots = stats[p]
                s = right_dot(kpad[pl.ds(ks, BK), lanes], qst[p])
                e = jnp.exp2(s * LOG2E + bias - lse)
                dp = right_dot(vpad[pl.ds(ks, BK), lanes], dst[p])
                ds = (e * (dp - dots)).astype(bf16)
                dv[pl.ds(ks, BK), lanes] += mm(e.astype(bf16), dst[p])
                dk[pl.ds(ks, BK), lanes] += mm(ds, qst[p])
                for h in range(2):
                    rows = slice(h * HEAD_DIM, (h + 1) * HEAD_DIM)
                    part = mm(
                        kt[p * PAIR + h * HEAD_DIM : p * PAIR + (h + 1) * HEAD_DIM, pl.ds(ks, BK)],
                        ds[:, h * BQ : (h + 1) * BQ],
                    )
                    acc[p, rows, :] = acc[p, rows, :] + part
            return 0

        lax.fori_loop(0, count_ref[i], k_step, 0)
        for p in range(pairs):
            out_ref[pl.ds(qs, BQ), p * PAIR : (p + 1) * PAIR] = (acc[p] * HEAD_DIM**-0.5).T.astype(bf16)
        return 0

    lax.fori_loop(0, full // BQ, q_step, 0)
    out_ref[:, width : 2 * width] = dk[0:full, :].astype(bf16)
    out_ref[:, 2 * width :] = dv[0:full, :].astype(bf16)


def smem():
    return pl.BlockSpec(memory_space=pltpu.SMEM)


def vmem():
    return pl.BlockSpec(memory_space=pltpu.VMEM)


def attend(qkv, tables):
    full, cols = qkv.shape
    width = cols // 3
    pairs = width // PAIR
    padded = full + BK - BQ
    starts, counts, kseg, qseg = tables
    return pl.pallas_call(
        forward_kernel,
        out_shape=(
            jax.ShapeDtypeStruct((full, width), bf16),
            jax.ShapeDtypeStruct((pairs, full // BQ, 2 * BQ), f32),
        ),
        in_specs=[smem(), smem(), vmem(), vmem(), vmem()],
        out_specs=(vmem(), vmem()),
        scratch_shapes=[
            pltpu.VMEM((padded, width), bf16),
            pltpu.VMEM((width, padded), bf16),
            pltpu.VMEM((pairs, 2 * BQ, PAIR), bf16),
            pltpu.VMEM((pairs, PAIR, BQ), f32),
        ],
        name="attn_fwd",
    )(starts, counts, qkv, kseg, qseg)


def attend_back(qkv, tables, ctx, lse, dctx):
    full, cols = qkv.shape
    width = cols // 3
    pairs = width // PAIR
    padded = full + BK - BQ
    starts, counts, kseg, qseg = tables
    return pl.pallas_call(
        backward_kernel,
        out_shape=jax.ShapeDtypeStruct((full, cols), bf16),
        in_specs=[smem(), smem()] + [vmem()] * 6,
        out_specs=vmem(),
        scratch_shapes=[
            pltpu.VMEM((padded, width), bf16),
            pltpu.VMEM((padded, width), bf16),
            pltpu.VMEM((width, padded), bf16),
            pltpu.VMEM((pairs, 2 * BQ, PAIR), bf16),
            pltpu.VMEM((pairs, 2 * BQ, PAIR), bf16),
            pltpu.VMEM((pairs, PAIR, BQ), f32),
            pltpu.VMEM((padded, width), f32),
            pltpu.VMEM((padded, width), f32),
        ],
        name="attn_bwd",
    )(starts, counts, qkv, kseg, qseg, ctx, lse, dctx)


def attention_tables(seg, valid):
    full = seg.shape[0]
    first = seg[::BQ]
    last = seg[BQ - 1 :: BQ]
    lo = jnp.sum((seg[None, :] < first[:, None]).astype(jnp.int32), axis=1)
    hi = jnp.sum((seg[None, :] <= last[:, None]).astype(jnp.int32), axis=1)
    starts = (lo // BQ) * BQ
    counts = (hi - starts + BK - 1) // BK
    keys = jnp.where(valid == 1, seg, -1)
    keys = jnp.concatenate([keys, jnp.full((BK - BQ,), -1, jnp.int32)])
    kseg = jnp.broadcast_to(keys[:, None], (full + BK - BQ, BQ))
    qseg = jnp.broadcast_to(seg[None, :], (8, full))
    return starts, counts, kseg, qseg


def norm_parts(values):
    center = jnp.mean(values, axis=-1, keepdims=True)
    centered = values - center
    spread = jnp.mean(centered * centered, axis=-1, keepdims=True)
    rate = lax.rsqrt(spread + 1e-06)
    return centered * rate, rate


def norm_back(grad, gain, n, rate):
    e = grad * gain
    return rate * (e - jnp.mean(e, axis=-1, keepdims=True) - n * jnp.mean(e * n, axis=-1, keepdims=True))


def swap(value):
    return lax.ppermute(value, "seq", [(0, 1), (1, 0)])


def per_device(
    layer_input,
    out_cotangent,
    gain1,
    shift1,
    w_qkv,
    bias_q,
    bias_v,
    w_out,
    bias_out,
    gain2,
    shift2,
    w_up,
    bias_up,
    w_down,
    bias_down,
    segment_ids,
    valid_mask,
):
    row_count, half, width = layer_input.shape
    full = 2 * half
    hw = width // 2
    side = lax.axis_index("seq")
    devices = lax.axis_size("rows") * 2
    is_low = side == 0

    def in_order(mine, other, axis):
        return jnp.where(
            is_low, jnp.concatenate([mine, other], axis=axis), jnp.concatenate([other, mine], axis=axis)
        )

    x_own = layer_input.reshape(half, width)
    x_peer = swap(x_own)
    tables = attention_tables(segment_ids.reshape(full), valid_mask.reshape(full))
    w_own = lax.dynamic_slice_in_dim(w_qkv.reshape(width, 3, width), side * hw, hw, axis=2).reshape(width, 3 * hw)
    bias_all = jnp.stack([bias_q, jnp.zeros_like(bias_q), bias_v])
    bias_own = lax.dynamic_slice_in_dim(bias_all, side * hw, hw, axis=1).reshape(3 * hw)

    n1, _ = norm_parts(in_order(x_own, x_peer, 0).astype(f32))
    normed1 = (n1 * gain1 + shift1).astype(bf16)
    qkv = (mm(normed1, w_own) + bias_own).astype(bf16)
    ctx_heads, lse = attend(qkv, tables)

    ctx_keep = lax.dynamic_slice_in_dim(ctx_heads, side * half, half, axis=0)
    ctx_peer = swap(lax.dynamic_slice_in_dim(ctx_heads, (1 - side) * half, half, axis=0))
    context = in_order(ctx_keep, ctx_peer, 1)
    inputs = x_own.astype(f32)
    hidden = inputs + mm(context, w_out) + bias_out
    n2, rate2 = norm_parts(hidden)
    normed2 = (n2 * gain2 + shift2).astype(bf16)
    upper = mm(normed2, w_up) + bias_up
    cdf = 0.5 * (1.0 + lax.erf(upper * (0.5**0.5)))
    act = (upper * cdf).astype(bf16)
    output = hidden + mm(act, w_down) + bias_down

    g_ffn = out_cotangent.reshape(half, width)
    g_wide = g_ffn.astype(f32)
    g_bias_down = jnp.sum(g_wide, axis=0)
    slope = cdf + upper * jnp.exp(-0.5 * upper * upper) * 0.3989422804014327
    g_upper = (right_dot(g_ffn, w_down) * slope).astype(bf16)
    g_normed2 = right_dot(g_upper, w_up)
    g_gain2 = jnp.sum(g_normed2 * n2, axis=0)
    g_shift2 = jnp.sum(g_normed2, axis=0)
    g_hidden = g_wide + norm_back(g_normed2, gain2, n2, rate2)
    g_attn = g_hidden.astype(bf16)

    w_out_peer = lax.dynamic_slice_in_dim(w_out, (1 - side) * hw, hw, axis=0)
    w_out_mine = lax.dynamic_slice_in_dim(w_out, side * hw, hw, axis=0)
    dctx_peer = swap(right_dot(g_attn, w_out_peer).astype(bf16))
    dctx_mine = right_dot(g_attn, w_out_mine).astype(bf16)

    g_w_down = left_dot(act, g_ffn).astype(bf16)
    g_w_up = left_dot(normed2, g_upper).astype(bf16)
    g_w_out = left_dot(context, g_attn).astype(bf16)
    g_bias_up = jnp.sum(g_upper.astype(f32), axis=0)
    g_bias_out = jnp.sum(g_attn.astype(f32), axis=0)

    both = ("rows", "seq")
    r_w_down = lax.psum_scatter(g_w_down, both, scatter_dimension=0, tiled=True)
    r_w_up = lax.psum_scatter(g_w_up, both, scatter_dimension=0, tiled=True)
    r_w_out = lax.psum_scatter(g_w_out, both, scatter_dimension=0, tiled=True)

    dctx = in_order(dctx_mine, dctx_peer, 0)
    g_qkv = attend_back(qkv, tables, ctx_heads, lse, dctx)

    g_part = right_dot(g_qkv, w_own)
    g_part_peer = swap(lax.dynamic_slice_in_dim(g_part, (1 - side) * half, half, axis=0).astype(bf16))
    g_part_keep = lax.dynamic_slice_in_dim(g_part, side * half, half, axis=0)

    blocks = left_dot(normed1, g_qkv).astype(bf16).reshape(devices // 2, 2, width // devices, 3 * hw)
    blocks_keep = lax.dynamic_index_in_dim(blocks, side, axis=1, keepdims=False)
    blocks_peer = swap(lax.dynamic_index_in_dim(blocks, 1 - side, axis=1, keepdims=False))
    merged = jnp.concatenate([blocks_keep, blocks_peer], axis=2)
    scattered = lax.psum_scatter(merged, "rows", scatter_dimension=0, tiled=True)
    scattered = scattered.reshape(width // devices, 2, 3, hw).astype(f32)
    r_w_qkv = in_order(scattered[:, 0], scattered[:, 1], 2).reshape(width // devices, 3 * width)

    g_gain1 = jnp.sum(g_part * n1, axis=0)
    g_shift1 = jnp.sum(g_part, axis=0)
    bias_sums = jnp.sum(g_qkv.astype(f32), axis=0)
    zero_half = jnp.zeros((hw,), f32)
    g_bias_q = in_order(bias_sums[:hw], zero_half, 0)
    g_bias_v = in_order(bias_sums[2 * hw :], zero_half, 0)

    vectors = (g_gain1, g_shift1, g_bias_q, g_bias_v, g_bias_out, g_gain2, g_shift2, g_bias_up, g_bias_down)
    packed = jnp.concatenate([v.reshape(devices, -1) for v in vectors], axis=1)
    packed = lax.psum_scatter(packed, both, scatter_dimension=0, tiled=True).reshape(-1)
    pieces = []
    at = 0
    for v in vectors:
        size = v.shape[0] // devices
        pieces.append(packed[at : at + size])
        at += size
    r_gain1, r_shift1, r_bias_q, r_bias_v, r_bias_out, r_gain2, r_shift2, r_bias_up, r_bias_down = pieces

    n1_own, rate1 = norm_parts(inputs)
    g_normed1 = g_part_keep + g_part_peer.astype(f32)
    grad_x = g_hidden + norm_back(g_normed1, gain1, n1_own, rate1)
    return (
        output.reshape(row_count, half, width),
        grad_x.reshape(row_count, half, width),
        r_gain1,
        r_shift1,
        r_w_qkv,
        r_bias_q,
        r_bias_v,
        r_w_out.astype(f32),
        r_bias_out,
        r_gain2,
        r_shift2,
        r_w_up.astype(f32),
        r_bias_up,
        r_w_down.astype(f32),
        r_bias_down,
    )


def solution(mesh):
    both = P(("rows", "seq"))
    both_wide = P(("rows", "seq"), None)
    tokens = P("rows", "seq", None)
    return jax.shard_map(
        per_device,
        mesh=mesh,
        in_specs=(tokens, tokens) + (P(),) * 13 + (P("rows", None), P("rows", None)),
        out_specs=(
            tokens,
            tokens,
            both,
            both,
            both_wide,
            both,
            both,
            both_wide,
            both,
            both,
            both,
            both_wide,
            both,
            both_wide,
            both,
        ),
        check_vma=False,
    )
```

```python
import functools

import jax
import jax.numpy as jnp
from jax import lax
from jax.experimental import pallas as pl
from jax.experimental.pallas import tpu as pltpu
from jax.sharding import PartitionSpec as P


HEAD_DIM = 64
BQ = 128
BK = 256
PAIR = 2 * HEAD_DIM
LOG2E = 1.4426950408889634
NEG = -1e30

f32 = jnp.float32
bf16 = jnp.bfloat16


def left_dot(left, right):
    return lax.dot_general(left, right, (((0,), (0,)), ((), ())), preferred_element_type=f32)


def right_dot(left, right):
    return lax.dot_general(left, right, (((1,), (1,)), ((), ())), preferred_element_type=f32)


def mm(left, right):
    return jnp.dot(left, right, preferred_element_type=f32)


def stack_heads(block):
    lane = lax.broadcasted_iota(jnp.int32, block.shape, 1)
    zero = jnp.zeros_like(block)
    return jnp.concatenate(
        [jnp.where(lane < HEAD_DIM, block, zero), jnp.where(lane < HEAD_DIM, zero, block)], axis=0
    )


def block_bias(kseg_ref, qseg_ref, qs, ks):
    same = kseg_ref[pl.ds(ks, BK), :] == qseg_ref[0:1, pl.ds(qs, BQ)]
    row = lax.broadcasted_iota(jnp.int32, (BK, BQ), 0)
    col = lax.broadcasted_iota(jnp.int32, (BK, BQ), 1)
    same = same | ((row - col) == (qs - ks))
    bias = jnp.where(same, 0.0, NEG)
    return jnp.concatenate([bias, bias], axis=1)


def gather_halves(dest, own_ref, peer_ref, side):
    half = own_ref.shape[0]
    own_at = side * half
    peer_at = half - own_at
    step = BQ // 2

    def move(i, _):
        at = pl.multiple_of(i * step, step)
        dest[pl.ds(pl.multiple_of(own_at + at, step), step), :] = own_ref[pl.ds(at, step), :]
        dest[pl.ds(pl.multiple_of(peer_at + at, step), step), :] = peer_ref[pl.ds(at, step), :]
        return 0

    lax.fori_loop(0, half // step, move, 0)


def copy_rows(dest_ref, source, start):
    step = BQ // 2

    def move(i, _):
        at = pl.multiple_of(i * step, step)
        dest_ref[pl.ds(at, step), :] = source[pl.ds(pl.multiple_of(start + at, step), step), :]
        return 0

    lax.fori_loop(0, dest_ref.shape[0] // step, move, 0)


def transpose_columns(dest, source, full, first, pairs):
    dest[:, full:] = jnp.zeros((dest.shape[0], dest.shape[1] - full), dest.dtype)

    def move(i, _):
        at = pl.multiple_of(i * BQ, BQ)
        for p in range(pairs):
            dest[p * PAIR : (p + 1) * PAIR, pl.ds(at, BQ)] = source[
                pl.ds(at, BQ), first + p * PAIR : first + (p + 1) * PAIR
            ].T
        return 0

    lax.fori_loop(0, full // BQ, move, 0)


def forward_kernel(second, side_ref, start_ref, count_ref, own_ref, peer_ref, kseg_ref, qseg_ref, *rest):
    if second:
        edge_in, lse_in, ctx_ref, lse_ref, qkv, ctx, vt, qst, acc = rest
    else:
        ctx_ref, edge_ref, lse_ref, qkv, ctx, vt, qst, acc = rest
    half, cols = own_ref.shape
    full = 2 * half
    width = cols // 3
    pairs = width // PAIR
    mid = half // BQ
    side = side_ref[0]
    gather_halves(qkv, own_ref, peer_ref, side)
    qkv[full:, :] = jnp.zeros((qkv.shape[0] - full, cols), bf16)
    transpose_columns(vt, qkv, full, 2 * width, pairs)
    edge_at = pl.multiple_of(mid * BQ + side * (BQ // 2), BQ // 2)
    if second:
        first_block = side * (mid + 1)
        last_block = first_block + mid
        lse_ref[...] = lse_in[...]
        ctx[pl.ds(edge_at, BQ // 2), :] = edge_in[...]
    else:
        first_block = (1 - side) * mid
        last_block = first_block + mid + 1
        lse_ref[...] = jnp.zeros(lse_ref.shape, f32)

    def q_step(i, _):
        qs = pl.multiple_of(i * BQ, BQ)
        start = start_ref[i]
        for p in range(pairs):
            blk = qkv[pl.ds(qs, BQ), p * PAIR : (p + 1) * PAIR]
            qst[p] = stack_heads(blk * jnp.asarray(HEAD_DIM**-0.5, bf16))
            acc[p] = jnp.zeros((PAIR, BQ), f32)

        def k_step(t, carry):
            ks = pl.multiple_of(start + t * BK, BQ)
            bias = block_bias(kseg_ref, qseg_ref, qs, ks)
            new = []
            for p in range(pairs):
                top, total = carry[p]
                s = right_dot(qkv[pl.ds(ks, BK), width + p * PAIR : width + (p + 1) * PAIR], qst[p])
                s = s * LOG2E + bias
                top_new = jnp.maximum(top, jnp.max(s, axis=0, keepdims=True))
                e = jnp.exp2(s - top_new)
                alpha = jnp.exp2(top - top_new)
                total = total * alpha + jnp.sum(e, axis=0, keepdims=True)
                e = e.astype(bf16)
                for h in range(2):
                    rows = slice(h * HEAD_DIM, (h + 1) * HEAD_DIM)
                    lanes = slice(h * BQ, (h + 1) * BQ)
                    part = mm(vt[p * PAIR + h * HEAD_DIM : p * PAIR + (h + 1) * HEAD_DIM, pl.ds(ks, BK)], e[:, lanes])
                    acc[p, rows, :] = acc[p, rows, :] * alpha[:, lanes] + part
                new.append((top_new, total))
            return tuple(new)

        init = tuple((jnp.full((1, 2 * BQ), NEG, f32), jnp.zeros((1, 2 * BQ), f32)) for _ in range(pairs))
        done = lax.fori_loop(0, count_ref[i], k_step, init)
        for p in range(pairs):
            top, total = done[p]
            inv = 1.0 / total
            parts = []
            for h in range(2):
                parts.append(acc[p, h * HEAD_DIM : (h + 1) * HEAD_DIM, :] * inv[:, h * BQ : (h + 1) * BQ])
            ctx[pl.ds(qs, BQ), p * PAIR : (p + 1) * PAIR] = jnp.concatenate(parts, axis=0).T.astype(bf16)
            lse_ref[p, pl.ds(i, 1), :] = top + jnp.log2(total)
        return 0

    lax.fori_loop(first_block, last_block, q_step, 0)
    if second:
        copy_rows(ctx_ref, ctx, side * half)
    else:
        copy_rows(ctx_ref, ctx, (1 - side) * half)
        edge_ref[...] = ctx[pl.ds(edge_at, BQ // 2), :]


def backward_kernel(
    side_ref,
    start_ref,
    count_ref,
    own_ref,
    peer_ref,
    kseg_ref,
    qseg_ref,
    ctx_own_ref,
    ctx_peer_ref,
    dctx_own_ref,
    dctx_peer_ref,
    lse_ref,
    out_own_ref,
    out_peer_ref,
    sums_ref,
    qkv,
    ctx,
    dctx,
    out,
    kt,
    qst,
    dst,
    acc,
    dk,
    dv,
):
    half, cols = own_ref.shape
    full = 2 * half
    width = cols // 3
    pairs = width // PAIR
    side = side_ref[0]
    gather_halves(qkv, own_ref, peer_ref, side)
    gather_halves(ctx, ctx_own_ref, ctx_peer_ref, side)
    gather_halves(dctx, dctx_own_ref, dctx_peer_ref, side)
    qkv[full:, :] = jnp.zeros((qkv.shape[0] - full, cols), bf16)
    transpose_columns(kt, qkv, full, width, pairs)

    def clear(i, _):
        at = pl.multiple_of(i * BQ, BQ)
        dk[pl.ds(at, BQ), :] = jnp.zeros((BQ, width), f32)
        dv[pl.ds(at, BQ), :] = jnp.zeros((BQ, width), f32)
        return 0

    lax.fori_loop(0, dk.shape[0] // BQ, clear, 0)
    head_row = lax.broadcasted_iota(jnp.int32, (8, PAIR), 0)
    head_lane = lax.broadcasted_iota(jnp.int32, (8, PAIR), 1) // HEAD_DIM
    pick = (head_row == head_lane).astype(f32)

    def q_step(i, _):
        qs = pl.multiple_of(i * BQ, BQ)
        start = start_ref[i]
        stats = []
        for p in range(pairs):
            lanes = slice(p * PAIR, (p + 1) * PAIR)
            blk = qkv[pl.ds(qs, BQ), lanes]
            qst[p] = stack_heads(blk * jnp.asarray(HEAD_DIM**-0.5, bf16))
            grad = dctx[pl.ds(qs, BQ), lanes]
            dst[p] = stack_heads(grad)
            acc[p] = jnp.zeros((PAIR, BQ), f32)
            prod = grad.astype(f32) * ctx[pl.ds(qs, BQ), lanes].astype(f32)
            dots = lax.dot_general(
                pick, prod, (((1,), (1,)), ((), ())), precision=lax.Precision.HIGHEST, preferred_element_type=f32
            )
            stats.append((lse_ref[p, pl.ds(i, 1), :], jnp.concatenate([dots[0:1], dots[1:2]], axis=1)))

        def k_step(t, _):
            ks = pl.multiple_of(start + t * BK, BQ)
            bias = block_bias(kseg_ref, qseg_ref, qs, ks)
            for p in range(pairs):
                lanes = slice(p * PAIR, (p + 1) * PAIR)
                lse, dots = stats[p]
                s = right_dot(qkv[pl.ds(ks, BK), width + p * PAIR : width + (p + 1) * PAIR], qst[p])
                e = jnp.exp2(s * LOG2E + bias - lse)
                dp = right_dot(qkv[pl.ds(ks, BK), 2 * width + p * PAIR : 2 * width + (p + 1) * PAIR], dst[p])
                ds = (e * (dp - dots)).astype(bf16)
                dv[pl.ds(ks, BK), lanes] += mm(e.astype(bf16), dst[p])
                dk[pl.ds(ks, BK), lanes] += mm(ds, qst[p])
                for h in range(2):
                    rows = slice(h * HEAD_DIM, (h + 1) * HEAD_DIM)
                    part = mm(
                        kt[p * PAIR + h * HEAD_DIM : p * PAIR + (h + 1) * HEAD_DIM, pl.ds(ks, BK)],
                        ds[:, h * BQ : (h + 1) * BQ],
                    )
                    acc[p, rows, :] = acc[p, rows, :] + part
            return 0

        lax.fori_loop(0, count_ref[i], k_step, 0)
        for p in range(pairs):
            out[pl.ds(qs, BQ), p * PAIR : (p + 1) * PAIR] = (acc[p] * HEAD_DIM**-0.5).T.astype(bf16)
        return 0

    lax.fori_loop(0, full // BQ, q_step, 0)

    def finish(i, sums):
        at = pl.multiple_of(i * BQ, BQ)
        out[pl.ds(at, BQ), width : 2 * width] = dk[pl.ds(at, BQ), :].astype(bf16)
        out[pl.ds(at, BQ), 2 * width :] = dv[pl.ds(at, BQ), :].astype(bf16)
        block = out[pl.ds(at, BQ), :].astype(f32).reshape(BQ // 8, 8, cols)
        return sums + jnp.sum(block, axis=0)

    sums_ref[...] = lax.fori_loop(0, full // BQ, finish, jnp.zeros((8, cols), f32))
    copy_rows(out_own_ref, out, side * half)
    copy_rows(out_peer_ref, out, (1 - side) * half)


def project_kernel(x_ref, gain_ref, shift_ref, w_ref, bias_ref, normed_ref, qkv_ref):
    n, _ = norm_parts(x_ref[...].astype(f32))
    normed = (n * gain_ref[...] + shift_ref[...]).astype(bf16)
    normed_ref[...] = normed
    qkv_ref[...] = (mm(normed, w_ref[...]) + bias_ref[...]).astype(bf16)


def project(x, gain, shift, w, bias):
    half, width = x.shape
    cols = w.shape[1]
    step = half // 4
    fixed = lambda i: (0, 0)
    moving = lambda i: (i, 0)
    return pl.pallas_call(
        project_kernel,
        grid=(4,),
        out_shape=(jax.ShapeDtypeStruct((half, width), bf16), jax.ShapeDtypeStruct((half, cols), bf16)),
        in_specs=[
            pl.BlockSpec((step, width), moving),
            pl.BlockSpec((1, width), fixed),
            pl.BlockSpec((1, width), fixed),
            pl.BlockSpec((width, cols), fixed),
            pl.BlockSpec((1, cols), fixed),
        ],
        out_specs=(pl.BlockSpec((step, width), moving), pl.BlockSpec((step, cols), moving)),
    )(x, gain[None], shift[None], w, bias[None])


def smem():
    return pl.BlockSpec(memory_space=pltpu.SMEM)


def vmem():
    return pl.BlockSpec(memory_space=pltpu.VMEM)


def attend(side, qkv_own, qkv_peer, tables, earlier=None):
    half, cols = qkv_own.shape
    full = 2 * half
    width = cols // 3
    pairs = width // PAIR
    padded = full + BK - BQ
    starts, counts, kseg, qseg = tables
    ctx_shape = jax.ShapeDtypeStruct((half, width), bf16)
    edge_shape = jax.ShapeDtypeStruct((BQ // 2, width), bf16)
    lse_shape = jax.ShapeDtypeStruct((pairs, full // BQ, 2 * BQ), f32)
    second = earlier is not None
    return pl.pallas_call(
        functools.partial(forward_kernel, second),
        out_shape=(ctx_shape, lse_shape) if second else (ctx_shape, edge_shape, lse_shape),
        in_specs=[smem()] * 3 + [vmem()] * (6 if second else 4),
        out_specs=(vmem(),) * (2 if second else 3),
        scratch_shapes=[
            pltpu.VMEM((padded, cols), bf16),
            pltpu.VMEM((full, width), bf16),
            pltpu.VMEM((width, padded), bf16),
            pltpu.VMEM((pairs, 2 * BQ, PAIR), bf16),
            pltpu.VMEM((pairs, PAIR, BQ), f32),
        ],
        name="attn_own" if second else "attn_peer",
    )(side, starts, counts, qkv_own, qkv_peer, kseg, qseg, *(earlier or ()))


def attend_back(side, qkv_own, qkv_peer, tables, ctx_own, ctx_peer, dctx_own, dctx_peer, lse):
    half, cols = qkv_own.shape
    full = 2 * half
    width = cols // 3
    pairs = width // PAIR
    padded = full + BK - BQ
    starts, counts, kseg, qseg = tables
    return pl.pallas_call(
        backward_kernel,
        out_shape=(
            jax.ShapeDtypeStruct((half, cols), bf16),
            jax.ShapeDtypeStruct((half, cols), bf16),
            jax.ShapeDtypeStruct((8, cols), f32),
        ),
        in_specs=[smem()] * 3 + [vmem()] * 9,
        out_specs=(vmem(),) * 3,
        scratch_shapes=[
            pltpu.VMEM((padded, cols), bf16),
            pltpu.VMEM((full, width), bf16),
            pltpu.VMEM((full, width), bf16),
            pltpu.VMEM((full, cols), bf16),
            pltpu.VMEM((width, padded), bf16),
            pltpu.VMEM((pairs, 2 * BQ, PAIR), bf16),
            pltpu.VMEM((pairs, 2 * BQ, PAIR), bf16),
            pltpu.VMEM((pairs, PAIR, BQ), f32),
            pltpu.VMEM((padded, width), f32),
            pltpu.VMEM((padded, width), f32),
        ],
        name="attn_bwd",
    )(side, starts, counts, qkv_own, qkv_peer, kseg, qseg, ctx_own, ctx_peer, dctx_own, dctx_peer, lse)


def attention_tables(seg, valid):
    full = seg.shape[0]
    first = seg[::BQ]
    last = seg[BQ - 1 :: BQ]
    lo = jnp.sum((seg[None, :] < first[:, None]).astype(jnp.int32), axis=1)
    hi = jnp.sum((seg[None, :] <= last[:, None]).astype(jnp.int32), axis=1)
    starts = (lo // BQ) * BQ
    counts = (hi - starts + BK - 1) // BK
    keys = jnp.where(valid == 1, seg, -1)
    keys = jnp.concatenate([keys, jnp.full((BK - BQ,), -1, jnp.int32)])
    kseg = jnp.broadcast_to(keys[:, None], (full + BK - BQ, BQ))
    qseg = jnp.broadcast_to(seg[None, :], (8, full))
    return starts, counts, kseg, qseg


def norm_parts(values):
    center = jnp.mean(values, axis=-1, keepdims=True)
    centered = values - center
    spread = jnp.mean(centered * centered, axis=-1, keepdims=True)
    rate = lax.rsqrt(spread + 1e-06)
    return centered * rate, rate


def norm_back(grad, gain, n, rate):
    e = grad * gain
    return rate * (e - jnp.mean(e, axis=-1, keepdims=True) - n * jnp.mean(e * n, axis=-1, keepdims=True))


def swap(value):
    return lax.ppermute(value, "seq", [(0, 1), (1, 0)])


def take(value, index, axis):
    return lax.dynamic_index_in_dim(value, index, axis=axis, keepdims=False)


class Place:
    def __init__(self):
        self.rows = lax.axis_size("rows")
        self.lines = self.rows // 4
        r = lax.axis_index("rows")
        self.side = lax.axis_index("seq")
        self.core = r % 2
        self.high = (r // 2) % 2
        self.line = r // 4

    def send(self, value, row_flip, side_flip):
        pairs = [
            (2 * r + s, 2 * (r ^ row_flip) + (s ^ side_flip)) for r in range(self.rows) for s in range(2)
        ]
        return lax.ppermute(value, ("rows", "seq"), pairs)

    def blocks(self, value):
        devices = 2 * self.rows
        return value.reshape((self.lines, 2, 2, 2, value.shape[0] // devices) + value.shape[1:])

    def core_stage(self, value):
        other = self.send(take(value, 1 - self.core, 2), 1, 0)
        return take(value, self.core, 2).astype(f32) + other.astype(f32)

    def plane_stage(self, value):
        got = [take(take(value, self.side, 2), self.high, 1)]
        for high, side in ((0, 1), (1, 0), (1, 1)):
            part = take(take(value, self.side ^ side, 2), self.high ^ high, 1)
            got.append(self.send(part, 2 * high, side))
        return [g.astype(f32) for g in got]

    def line_stage(self, value):
        total = take(value, self.line, 0).astype(f32)
        for step in range(1, self.lines):
            total = total + self.send(take(value, self.line ^ step, 0), 4 * step, 0).astype(f32)
        return total


def per_device(
    layer_input,
    out_cotangent,
    gain1,
    shift1,
    w_qkv,
    bias_q,
    bias_v,
    w_out,
    bias_out,
    gain2,
    shift2,
    w_up,
    bias_up,
    w_down,
    bias_down,
    segment_ids,
    valid_mask,
):
    row_count, half, width = layer_input.shape
    full = 2 * half
    hw = width // 2
    side = lax.axis_index("seq")
    devices = lax.axis_size("rows") * 2
    is_low = side == 0

    def in_order(mine, other, axis):
        return jnp.where(
            is_low, jnp.concatenate([mine, other], axis=axis), jnp.concatenate([other, mine], axis=axis)
        )

    def side_columns(value, low):
        parts = []
        for at in range(0, value.shape[-1], width):
            parts.append(jnp.where(low, value[..., at : at + hw], value[..., at + hw : at + width]))
        return jnp.concatenate(parts, axis=-1)

    x_own = layer_input.reshape(half, width)
    x_peer = swap(x_own)
    tables = attention_tables(segment_ids.reshape(full), valid_mask.reshape(full))
    w_own = side_columns(w_qkv, is_low)
    bias_own = side_columns(jnp.concatenate([bias_q, jnp.zeros_like(bias_q), bias_v]), is_low)
    side_ref = side.reshape(1).astype(jnp.int32)

    normed1_own, qkv_own = project(x_own, gain1, shift1, w_own, bias_own)
    normed1_peer, qkv_peer = project(x_peer, gain1, shift1, w_own, bias_own)
    ctx_peer, ctx_edge, lse = attend(side_ref, qkv_own, qkv_peer, tables)
    ctx_got = swap(ctx_peer)
    ctx_own, lse = attend(side_ref, qkv_own, qkv_peer, tables, (ctx_edge, lse))

    context = in_order(ctx_own, ctx_got, 1)
    inputs = x_own.astype(f32)
    hidden = inputs + mm(context, w_out) + bias_out
    n2, rate2 = norm_parts(hidden)
    normed2 = (n2 * gain2 + shift2).astype(bf16)
    upper = mm(normed2, w_up) + bias_up
    cdf = 0.5 * (1.0 + lax.erf(upper * (0.5**0.5)))
    act = (upper * cdf).astype(bf16)
    output = hidden + mm(act, w_down) + bias_down

    g_ffn = out_cotangent.reshape(half, width)
    g_wide = g_ffn.astype(f32)
    g_bias_down = jnp.sum(g_wide, axis=0)
    slope = cdf + upper * jnp.exp(-0.5 * upper * upper) * 0.3989422804014327
    g_upper = (right_dot(g_ffn, w_down) * slope).astype(bf16)
    g_normed2 = right_dot(g_upper, w_up)
    g_gain2 = jnp.sum(g_normed2 * n2, axis=0)
    g_shift2 = jnp.sum(g_normed2, axis=0)
    g_hidden = g_wide + norm_back(g_normed2, gain2, n2, rate2)
    g_attn = g_hidden.astype(bf16)

    w_out_mine = jnp.where(is_low, w_out[:hw], w_out[hw:])
    w_out_peer = jnp.where(is_low, w_out[hw:], w_out[:hw])
    dctx_peer = swap(right_dot(g_attn, w_out_peer).astype(bf16))
    dctx_mine = right_dot(g_attn, w_out_mine).astype(bf16)

    g_w_down = left_dot(act, g_ffn).astype(bf16)
    g_w_up = left_dot(normed2, g_upper).astype(bf16)
    g_w_out = left_dot(context, g_attn).astype(bf16)
    g_bias_up = jnp.sum(g_upper.astype(f32), axis=0)
    g_bias_out = jnp.sum(g_attn.astype(f32), axis=0)

    place = Place()
    first = place.core_stage(place.blocks(g_w_down))
    second = place.core_stage(place.blocks(g_w_up))
    third = place.core_stage(place.blocks(g_w_out))
    wide = g_w_up.shape[1] // width
    parts = [first] + [second[..., c * width : (c + 1) * width] for c in range(wide)] + [third]
    ffn = jnp.concatenate(parts, axis=-2).astype(bf16)
    dctx_peer, ffn = lax.optimization_barrier((dctx_peer, ffn))
    ffn_parts = place.plane_stage(ffn)
    g_own, g_peer, g_sums = attend_back(
        side_ref, qkv_own, qkv_peer, tables, ctx_own, ctx_peer, dctx_mine, dctx_peer, lse
    )
    ffn = ((ffn_parts[0] + ffn_parts[1]) + (ffn_parts[2] + ffn_parts[3])).astype(bf16)
    ffn = place.line_stage(ffn)
    n_down = g_w_down.shape[0] // devices
    n_row = width // devices
    r_w_down = ffn[:n_down]
    r_w_up = jnp.concatenate(
        [ffn[n_down + c * n_row : n_down + (c + 1) * n_row] for c in range(wide)], axis=1
    )
    r_w_out = ffn[n_down + wide * n_row :]

    g_part_peer = right_dot(g_peer, w_own).astype(bf16)
    g_part_got = swap(g_part_peer)
    g_w_qkv = left_dot(normed1_own, g_own) + left_dot(normed1_peer, g_peer)
    core_w_qkv = place.core_stage(place.blocks(g_w_qkv.astype(bf16)))
    g_part_own = right_dot(g_own, w_own)

    bias_sums = jnp.sum(g_sums, axis=0)
    w_wide = w_own.astype(f32)
    g_shift1 = jnp.sum(w_wide * bias_sums, axis=1)
    g_gain1 = (jnp.sum(w_wide * g_w_qkv, axis=1) - shift1 * g_shift1) / gain1
    zero_half = jnp.zeros((hw,), f32)
    g_bias_q = in_order(bias_sums[:hw], zero_half, 0)
    g_bias_v = in_order(bias_sums[2 * hw :], zero_half, 0)
    vectors = (g_gain1, g_shift1, g_bias_q, g_bias_v, g_bias_out, g_gain2, g_shift2, g_bias_down)
    packed = [v.reshape(devices, n_row, 1) for v in vectors]
    packed.append(jnp.swapaxes(g_bias_up.reshape(devices, wide, n_row), 1, 2))
    packed = jnp.concatenate(packed, axis=2)
    columns = packed.shape[2]
    coarse = packed.astype(bf16)
    fine = (packed - coarse.astype(f32)).astype(bf16)
    lanes = jnp.zeros((devices, n_row, 128 - 2 * columns), bf16)
    lanes = jnp.concatenate([coarse, fine, lanes], axis=2).reshape(width, 128)

    core_lanes = place.core_stage(place.blocks(lanes))
    tail_wide = 3 * hw

    def resplit(value):
        sums = value[..., :columns] + value[..., columns : 2 * columns]
        high = sums.astype(bf16)
        low = (sums - high.astype(f32)).astype(bf16)
        return jnp.concatenate([high, low, value[..., 2 * columns :].astype(bf16)], axis=-1)

    tail = jnp.concatenate([core_w_qkv.astype(bf16), resplit(core_lanes)], axis=-1)
    kept, across, above, beyond = place.plane_stage(tail)
    mine = (kept + above)[..., :tail_wide]
    theirs = (across + beyond)[..., :tail_wide]
    sums = ((kept + across) + (above + beyond))[..., tail_wide:]
    tail = jnp.concatenate([mine.astype(bf16), theirs.astype(bf16), resplit(sums)], axis=-1)
    tail = place.line_stage(tail)
    r_w_qkv = in_order(
        tail[:, :tail_wide].reshape(n_row, 3, hw), tail[:, tail_wide : 2 * tail_wide].reshape(n_row, 3, hw), 2
    ).reshape(n_row, 3 * width)
    sums = tail[:, 2 * tail_wide : 2 * tail_wide + columns] + tail[:, 2 * tail_wide + columns : 2 * tail_wide + 2 * columns]
    sums = sums.T
    r_gain1, r_shift1, r_bias_q, r_bias_v, r_bias_out, r_gain2, r_shift2, r_bias_down = [sums[k] for k in range(8)]
    r_bias_up = sums[8:].reshape(wide * n_row)

    n1_own, rate1 = norm_parts(inputs)
    g_normed1 = g_part_own + g_part_got.astype(f32)
    grad_x = g_hidden + norm_back(g_normed1, gain1, n1_own, rate1)
    return (
        output.reshape(row_count, half, width),
        grad_x.reshape(row_count, half, width),
        r_gain1,
        r_shift1,
        r_w_qkv,
        r_bias_q,
        r_bias_v,
        r_w_out,
        r_bias_out,
        r_gain2,
        r_shift2,
        r_w_up,
        r_bias_up,
        r_w_down,
        r_bias_down,
    )


def solution(mesh):
    both = P(("rows", "seq"))
    both_wide = P(("rows", "seq"), None)
    tokens = P("rows", "seq", None)

    return jax.shard_map(
        per_device,
        mesh=mesh,
        in_specs=(tokens, tokens) + (P(),) * 13 + (P("rows", None), P("rows", None)),
        out_specs=(
            tokens,
            tokens,
            both,
            both,
            both_wide,
            both,
            both,
            both_wide,
            both,
            both,
            both,
            both_wide,
            both,
            both_wide,
            both,
        ),
        check_vma=False,
    )
```

```python
import functools

import jax
import jax.numpy as jnp
from jax import lax
from jax.experimental import pallas as pl
from jax.experimental.pallas import tpu as pltpu
from jax.sharding import PartitionSpec as P


HEAD_DIM = 64
BQ = 128
BK = 512
PAIR = 2 * HEAD_DIM
LOG2E = 1.4426950408889634
NEG = -1e30

f32 = jnp.float32
bf16 = jnp.bfloat16


def left_dot(left, right):
    return lax.dot_general(left, right, (((0,), (0,)), ((), ())), preferred_element_type=f32)


def right_dot(left, right):
    return lax.dot_general(left, right, (((1,), (1,)), ((), ())), preferred_element_type=f32)


def mm(left, right):
    return jnp.dot(left, right, preferred_element_type=f32)


def stack_heads(block):
    lane = lax.broadcasted_iota(jnp.int32, block.shape, 1)
    zero = jnp.zeros_like(block)
    return jnp.concatenate(
        [jnp.where(lane < HEAD_DIM, block, zero), jnp.where(lane < HEAD_DIM, zero, block)], axis=0
    )


def block_bias(kseg_ref, qseg_ref, qs, ks):
    same = kseg_ref[pl.ds(ks, BK), :] == qseg_ref[0:1, pl.ds(qs, BQ)]
    row = lax.broadcasted_iota(jnp.int32, (BK, BQ), 0)
    col = lax.broadcasted_iota(jnp.int32, (BK, BQ), 1)
    same = same | ((row - col) == (qs - ks))
    bias = jnp.where(same, 0.0, NEG)
    return jnp.concatenate([bias, bias], axis=1)


def gather_halves(dest, own_ref, peer_ref, side):
    half = own_ref.shape[0]
    own_at = side * half
    peer_at = half - own_at
    step = BQ // 2

    def move(i, _):
        at = pl.multiple_of(i * step, step)
        dest[pl.ds(pl.multiple_of(own_at + at, step), step), :] = own_ref[pl.ds(at, step), :]
        dest[pl.ds(pl.multiple_of(peer_at + at, step), step), :] = peer_ref[pl.ds(at, step), :]
        return 0

    lax.fori_loop(0, half // step, move, 0)


def copy_rows(dest_ref, source, start):
    step = BQ // 2

    def move(i, _):
        at = pl.multiple_of(i * step, step)
        dest_ref[pl.ds(at, step), :] = source[pl.ds(pl.multiple_of(start + at, step), step), :]
        return 0

    lax.fori_loop(0, dest_ref.shape[0] // step, move, 0)


def transpose_columns(dest, source, full, first, pairs):
    dest[:, full:] = jnp.zeros((dest.shape[0], dest.shape[1] - full), dest.dtype)

    def move(i, _):
        at = pl.multiple_of(i * BQ, BQ)
        for p in range(pairs):
            dest[p * PAIR : (p + 1) * PAIR, pl.ds(at, BQ)] = source[
                pl.ds(at, BQ), first + p * PAIR : first + (p + 1) * PAIR
            ].T
        return 0

    lax.fori_loop(0, full // BQ, move, 0)


def forward_kernel(second, side_ref, start_ref, count_ref, own_ref, peer_ref, kseg_ref, qseg_ref, *rest):
    if second:
        edge_in, lse_in, ctx_ref, lse_ref, qkv, ctx, vt, qst, acc = rest
    else:
        ctx_ref, edge_ref, lse_ref, qkv, ctx, vt, qst, acc = rest
    half, cols = own_ref.shape
    full = 2 * half
    width = cols // 3
    pairs = width // PAIR
    mid = half // BQ
    side = side_ref[0]
    gather_halves(qkv, own_ref, peer_ref, side)
    qkv[full:, :] = jnp.zeros((qkv.shape[0] - full, cols), bf16)
    transpose_columns(vt, qkv, full, 2 * width, pairs)
    edge_at = pl.multiple_of(mid * BQ + side * (BQ // 2), BQ // 2)
    if second:
        first_block = side * (mid + 1)
        last_block = first_block + mid
        lse_ref[...] = lse_in[...]
        ctx[pl.ds(edge_at, BQ // 2), :] = edge_in[...]
    else:
        first_block = (1 - side) * mid
        last_block = first_block + mid + 1
        lse_ref[...] = jnp.zeros(lse_ref.shape, f32)

    def q_step(i, _):
        qs = pl.multiple_of(i * BQ, BQ)
        start = start_ref[i]
        for p in range(pairs):
            blk = qkv[pl.ds(qs, BQ), p * PAIR : (p + 1) * PAIR]
            qst[p] = stack_heads(blk * jnp.asarray(HEAD_DIM**-0.5, bf16))
            acc[p] = jnp.zeros((PAIR, BQ), f32)

        def k_step(t, carry):
            ks = pl.multiple_of(start + t * BK, BQ)
            bias = block_bias(kseg_ref, qseg_ref, qs, ks)
            new = []
            for p in range(pairs):
                top, total = carry[p]
                s = right_dot(qkv[pl.ds(ks, BK), width + p * PAIR : width + (p + 1) * PAIR], qst[p])
                s = s * LOG2E + bias
                top_new = jnp.maximum(top, jnp.max(s, axis=0, keepdims=True))
                e = jnp.exp2(s - top_new)
                alpha = jnp.exp2(top - top_new)
                total = total * alpha + jnp.sum(e, axis=0, keepdims=True)
                e = e.astype(bf16)
                for h in range(2):
                    rows = slice(h * HEAD_DIM, (h + 1) * HEAD_DIM)
                    lanes = slice(h * BQ, (h + 1) * BQ)
                    part = mm(vt[p * PAIR + h * HEAD_DIM : p * PAIR + (h + 1) * HEAD_DIM, pl.ds(ks, BK)], e[:, lanes])
                    acc[p, rows, :] = acc[p, rows, :] * alpha[:, lanes] + part
                new.append((top_new, total))
            return tuple(new)

        init = tuple((jnp.full((1, 2 * BQ), NEG, f32), jnp.zeros((1, 2 * BQ), f32)) for _ in range(pairs))
        done = lax.fori_loop(0, count_ref[i], k_step, init)
        for p in range(pairs):
            top, total = done[p]
            inv = 1.0 / total
            parts = []
            for h in range(2):
                parts.append(acc[p, h * HEAD_DIM : (h + 1) * HEAD_DIM, :] * inv[:, h * BQ : (h + 1) * BQ])
            ctx[pl.ds(qs, BQ), p * PAIR : (p + 1) * PAIR] = jnp.concatenate(parts, axis=0).T.astype(bf16)
            lse_ref[p, pl.ds(i, 1), :] = top + jnp.log2(total)
        return 0

    lax.fori_loop(first_block, last_block, q_step, 0)
    if second:
        copy_rows(ctx_ref, ctx, side * half)
    else:
        copy_rows(ctx_ref, ctx, (1 - side) * half)
        edge_ref[...] = ctx[pl.ds(edge_at, BQ // 2), :]


def backward_kernel(
    side_ref,
    start_ref,
    count_ref,
    own_ref,
    peer_ref,
    kseg_ref,
    qseg_ref,
    ctx_own_ref,
    ctx_peer_ref,
    dctx_own_ref,
    dctx_peer_ref,
    lse_ref,
    out_own_ref,
    out_peer_ref,
    sums_ref,
    qkv,
    ctx,
    dctx,
    out,
    kt,
    qst,
    dst,
    acc,
    dk,
    dv,
):
    half, cols = own_ref.shape
    full = 2 * half
    width = cols // 3
    pairs = width // PAIR
    side = side_ref[0]
    gather_halves(qkv, own_ref, peer_ref, side)
    gather_halves(ctx, ctx_own_ref, ctx_peer_ref, side)
    gather_halves(dctx, dctx_own_ref, dctx_peer_ref, side)
    qkv[full:, :] = jnp.zeros((qkv.shape[0] - full, cols), bf16)
    transpose_columns(kt, qkv, full, width, pairs)

    def clear(i, _):
        at = pl.multiple_of(i * BQ, BQ)
        dk[pl.ds(at, BQ), :] = jnp.zeros((BQ, width), f32)
        dv[pl.ds(at, BQ), :] = jnp.zeros((BQ, width), f32)
        return 0

    lax.fori_loop(0, dk.shape[0] // BQ, clear, 0)
    head_row = lax.broadcasted_iota(jnp.int32, (8, PAIR), 0)
    head_lane = lax.broadcasted_iota(jnp.int32, (8, PAIR), 1) // HEAD_DIM
    pick = (head_row == head_lane).astype(f32)

    def q_step(i, _):
        qs = pl.multiple_of(i * BQ, BQ)
        start = start_ref[i]
        stats = []
        for p in range(pairs):
            lanes = slice(p * PAIR, (p + 1) * PAIR)
            blk = qkv[pl.ds(qs, BQ), lanes]
            qst[p] = stack_heads(blk * jnp.asarray(HEAD_DIM**-0.5, bf16))
            grad = dctx[pl.ds(qs, BQ), lanes]
            dst[p] = stack_heads(grad)
            acc[p] = jnp.zeros((PAIR, BQ), f32)
            prod = grad.astype(f32) * ctx[pl.ds(qs, BQ), lanes].astype(f32)
            dots = lax.dot_general(
                pick, prod, (((1,), (1,)), ((), ())), precision=lax.Precision.HIGHEST, preferred_element_type=f32
            )
            stats.append((lse_ref[p, pl.ds(i, 1), :], jnp.concatenate([dots[0:1], dots[1:2]], axis=1)))

        def k_step(t, _):
            ks = pl.multiple_of(start + t * BK, BQ)
            bias = block_bias(kseg_ref, qseg_ref, qs, ks)
            for p in range(pairs):
                lanes = slice(p * PAIR, (p + 1) * PAIR)
                lse, dots = stats[p]
                s = right_dot(qkv[pl.ds(ks, BK), width + p * PAIR : width + (p + 1) * PAIR], qst[p])
                e = jnp.exp2(s * LOG2E + bias - lse)
                dp = right_dot(qkv[pl.ds(ks, BK), 2 * width + p * PAIR : 2 * width + (p + 1) * PAIR], dst[p])
                ds = (e * (dp - dots)).astype(bf16)
                dv[pl.ds(ks, BK), lanes] += mm(e.astype(bf16), dst[p])
                dk[pl.ds(ks, BK), lanes] += mm(ds, qst[p])
                for h in range(2):
                    rows = slice(h * HEAD_DIM, (h + 1) * HEAD_DIM)
                    part = mm(
                        kt[p * PAIR + h * HEAD_DIM : p * PAIR + (h + 1) * HEAD_DIM, pl.ds(ks, BK)],
                        ds[:, h * BQ : (h + 1) * BQ],
                    )
                    acc[p, rows, :] = acc[p, rows, :] + part
            return 0

        lax.fori_loop(0, count_ref[i], k_step, 0)
        for p in range(pairs):
            out[pl.ds(qs, BQ), p * PAIR : (p + 1) * PAIR] = (acc[p] * HEAD_DIM**-0.5).T.astype(bf16)
        return 0

    lax.fori_loop(0, full // BQ, q_step, 0)

    def finish(i, sums):
        at = pl.multiple_of(i * BQ, BQ)
        out[pl.ds(at, BQ), width : 2 * width] = dk[pl.ds(at, BQ), :].astype(bf16)
        out[pl.ds(at, BQ), 2 * width :] = dv[pl.ds(at, BQ), :].astype(bf16)
        block = out[pl.ds(at, BQ), :].astype(f32).reshape(BQ // 8, 8, cols)
        return sums + jnp.sum(block, axis=0)

    sums_ref[...] = lax.fori_loop(0, full // BQ, finish, jnp.zeros((8, cols), f32))
    copy_rows(out_own_ref, out, side * half)
    copy_rows(out_peer_ref, out, (1 - side) * half)


def project_kernel(x_ref, gain_ref, shift_ref, w_ref, bias_ref, normed_ref, qkv_ref):
    n, _ = norm_parts(x_ref[...].astype(f32))
    normed = (n * gain_ref[...] + shift_ref[...]).astype(bf16)
    normed_ref[...] = normed
    qkv_ref[...] = (mm(normed, w_ref[...]) + bias_ref[...]).astype(bf16)


def project(x, gain, shift, w, bias):
    half, width = x.shape
    cols = w.shape[1]
    step = half // 4
    fixed = lambda i: (0, 0)
    moving = lambda i: (i, 0)
    return pl.pallas_call(
        project_kernel,
        grid=(4,),
        out_shape=(jax.ShapeDtypeStruct((half, width), bf16), jax.ShapeDtypeStruct((half, cols), bf16)),
        in_specs=[
            pl.BlockSpec((step, width), moving),
            pl.BlockSpec((1, width), fixed),
            pl.BlockSpec((1, width), fixed),
            pl.BlockSpec((width, cols), fixed),
            pl.BlockSpec((1, cols), fixed),
        ],
        out_specs=(pl.BlockSpec((step, width), moving), pl.BlockSpec((step, cols), moving)),
    )(x, gain[None], shift[None], w, bias[None])


def smem():
    return pl.BlockSpec(memory_space=pltpu.SMEM)


def vmem():
    return pl.BlockSpec(memory_space=pltpu.VMEM)


def attend(side, qkv_own, qkv_peer, tables, earlier=None):
    half, cols = qkv_own.shape
    full = 2 * half
    width = cols // 3
    pairs = width // PAIR
    padded = full + BK - BQ
    starts, counts, kseg, qseg = tables
    ctx_shape = jax.ShapeDtypeStruct((half, width), bf16)
    edge_shape = jax.ShapeDtypeStruct((BQ // 2, width), bf16)
    lse_shape = jax.ShapeDtypeStruct((pairs, full // BQ, 2 * BQ), f32)
    second = earlier is not None
    return pl.pallas_call(
        functools.partial(forward_kernel, second),
        out_shape=(ctx_shape, lse_shape) if second else (ctx_shape, edge_shape, lse_shape),
        in_specs=[smem()] * 3 + [vmem()] * (6 if second else 4),
        out_specs=(vmem(),) * (2 if second else 3),
        scratch_shapes=[
            pltpu.VMEM((padded, cols), bf16),
            pltpu.VMEM((full, width), bf16),
            pltpu.VMEM((width, padded), bf16),
            pltpu.VMEM((pairs, 2 * BQ, PAIR), bf16),
            pltpu.VMEM((pairs, PAIR, BQ), f32),
        ],
        name="attn_own" if second else "attn_peer",
    )(side, starts, counts, qkv_own, qkv_peer, kseg, qseg, *(earlier or ()))


def attend_back(side, qkv_own, qkv_peer, tables, ctx_own, ctx_peer, dctx_own, dctx_peer, lse):
    half, cols = qkv_own.shape
    full = 2 * half
    width = cols // 3
    pairs = width // PAIR
    padded = full + BK - BQ
    starts, counts, kseg, qseg = tables
    return pl.pallas_call(
        backward_kernel,
        out_shape=(
            jax.ShapeDtypeStruct((half, cols), bf16),
            jax.ShapeDtypeStruct((half, cols), bf16),
            jax.ShapeDtypeStruct((8, cols), f32),
        ),
        in_specs=[smem()] * 3 + [vmem()] * 9,
        out_specs=(vmem(),) * 3,
        scratch_shapes=[
            pltpu.VMEM((padded, cols), bf16),
            pltpu.VMEM((full, width), bf16),
            pltpu.VMEM((full, width), bf16),
            pltpu.VMEM((full, cols), bf16),
            pltpu.VMEM((width, padded), bf16),
            pltpu.VMEM((pairs, 2 * BQ, PAIR), bf16),
            pltpu.VMEM((pairs, 2 * BQ, PAIR), bf16),
            pltpu.VMEM((pairs, PAIR, BQ), f32),
            pltpu.VMEM((padded, width), f32),
            pltpu.VMEM((padded, width), f32),
        ],
        name="attn_bwd",
    )(side, starts, counts, qkv_own, qkv_peer, kseg, qseg, ctx_own, ctx_peer, dctx_own, dctx_peer, lse)


def attention_tables(seg, valid):
    full = seg.shape[0]
    first = seg[::BQ]
    last = seg[BQ - 1 :: BQ]
    lo = jnp.sum((seg[None, :] < first[:, None]).astype(jnp.int32), axis=1)
    hi = jnp.sum((seg[None, :] <= last[:, None]).astype(jnp.int32), axis=1)
    starts = (lo // BQ) * BQ
    counts = (hi - starts + BK - 1) // BK
    keys = jnp.where(valid == 1, seg, -1)
    keys = jnp.concatenate([keys, jnp.full((BK - BQ,), -1, jnp.int32)])
    kseg = jnp.broadcast_to(keys[:, None], (full + BK - BQ, BQ))
    qseg = jnp.broadcast_to(seg[None, :], (8, full))
    return starts, counts, kseg, qseg


def norm_parts(values):
    center = jnp.mean(values, axis=-1, keepdims=True)
    centered = values - center
    spread = jnp.mean(centered * centered, axis=-1, keepdims=True)
    rate = lax.rsqrt(spread + 1e-06)
    return centered * rate, rate


def norm_back(grad, gain, n, rate):
    e = grad * gain
    return rate * (e - jnp.mean(e, axis=-1, keepdims=True) - n * jnp.mean(e * n, axis=-1, keepdims=True))


def swap(value):
    return lax.ppermute(value, "seq", [(0, 1), (1, 0)])


def take(value, index, axis):
    return lax.dynamic_index_in_dim(value, index, axis=axis, keepdims=False)


class Place:
    def __init__(self):
        self.rows = lax.axis_size("rows")
        self.lines = self.rows // 4
        r = lax.axis_index("rows")
        self.side = lax.axis_index("seq")
        self.core = r % 2
        self.high = (r // 2) % 2
        self.line = r // 4

    def send(self, value, row_flip, side_flip):
        pairs = [
            (2 * r + s, 2 * (r ^ row_flip) + (s ^ side_flip)) for r in range(self.rows) for s in range(2)
        ]
        return lax.ppermute(value, ("rows", "seq"), pairs)

    def blocks(self, value):
        devices = 2 * self.rows
        return value.reshape((self.lines, 2, 2, 2, value.shape[0] // devices) + value.shape[1:])

    def core_stage(self, value):
        other = self.send(take(value, 1 - self.core, 2), 1, 0)
        return take(value, self.core, 2).astype(f32) + other.astype(f32)

    def plane_stage(self, value):
        got = [take(take(value, self.side, 2), self.high, 1)]
        for high, side in ((0, 1), (1, 0), (1, 1)):
            part = take(take(value, self.side ^ side, 2), self.high ^ high, 1)
            got.append(self.send(part, 2 * high, side))
        return [g.astype(f32) for g in got]

    def line_stage(self, value):
        total = take(value, self.line, 0).astype(f32)
        for step in range(1, self.lines):
            total = total + self.send(take(value, self.line ^ step, 0), 4 * step, 0).astype(f32)
        return total


def per_device(
    layer_input,
    out_cotangent,
    gain1,
    shift1,
    w_qkv,
    bias_q,
    bias_v,
    w_out,
    bias_out,
    gain2,
    shift2,
    w_up,
    bias_up,
    w_down,
    bias_down,
    segment_ids,
    valid_mask,
):
    row_count, half, width = layer_input.shape
    full = 2 * half
    hw = width // 2
    side = lax.axis_index("seq")
    devices = lax.axis_size("rows") * 2
    is_low = side == 0

    def in_order(mine, other, axis):
        return jnp.where(
            is_low, jnp.concatenate([mine, other], axis=axis), jnp.concatenate([other, mine], axis=axis)
        )

    def side_columns(value, low):
        parts = []
        for at in range(0, value.shape[-1], width):
            parts.append(jnp.where(low, value[..., at : at + hw], value[..., at + hw : at + width]))
        return jnp.concatenate(parts, axis=-1)

    x_own = layer_input.reshape(half, width)
    x_peer = swap(x_own)
    tables = attention_tables(segment_ids.reshape(full), valid_mask.reshape(full))
    w_own = side_columns(w_qkv, is_low)
    bias_own = side_columns(jnp.concatenate([bias_q, jnp.zeros_like(bias_q), bias_v]), is_low)
    side_ref = side.reshape(1).astype(jnp.int32)

    normed1_own, qkv_own = project(x_own, gain1, shift1, w_own, bias_own)
    normed1_peer, qkv_peer = project(x_peer, gain1, shift1, w_own, bias_own)
    ctx_peer, ctx_edge, lse = attend(side_ref, qkv_own, qkv_peer, tables)
    ctx_got = swap(ctx_peer)
    ctx_own, lse = attend(side_ref, qkv_own, qkv_peer, tables, (ctx_edge, lse))

    context = in_order(ctx_own, ctx_got, 1)
    inputs = x_own.astype(f32)
    hidden = inputs + mm(context, w_out) + bias_out
    n2, rate2 = norm_parts(hidden)
    normed2 = (n2 * gain2 + shift2).astype(bf16)
    upper = mm(normed2, w_up) + bias_up
    cdf = 0.5 * (1.0 + lax.erf(upper * (0.5**0.5)))
    act = (upper * cdf).astype(bf16)
    output = hidden + mm(act, w_down) + bias_down

    g_ffn = out_cotangent.reshape(half, width)
    g_wide = g_ffn.astype(f32)
    g_bias_down = jnp.sum(g_wide, axis=0)
    slope = cdf + upper * jnp.exp(-0.5 * upper * upper) * 0.3989422804014327
    g_upper = (right_dot(g_ffn, w_down) * slope).astype(bf16)
    g_normed2 = right_dot(g_upper, w_up)
    g_gain2 = jnp.sum(g_normed2 * n2, axis=0)
    g_shift2 = jnp.sum(g_normed2, axis=0)
    g_hidden = g_wide + norm_back(g_normed2, gain2, n2, rate2)
    g_attn = g_hidden.astype(bf16)

    w_out_mine = jnp.where(is_low, w_out[:hw], w_out[hw:])
    w_out_peer = jnp.where(is_low, w_out[hw:], w_out[:hw])
    dctx_part = right_dot(g_attn, w_out_peer).astype(bf16)
    dctx_peer = swap(dctx_part)
    dctx_mine = right_dot(g_attn, w_out_mine).astype(bf16)

    g_w_down = left_dot(act, g_ffn).astype(bf16)
    g_w_up = left_dot(normed2, g_upper).astype(bf16)
    g_w_out = left_dot(context, g_attn).astype(bf16)
    g_bias_up = jnp.sum(g_upper.astype(f32), axis=0)
    g_bias_out = jnp.sum(g_attn.astype(f32), axis=0)

    place = Place()
    first = place.core_stage(place.blocks(g_w_down))
    second = place.core_stage(place.blocks(g_w_up))
    third = place.core_stage(place.blocks(g_w_out))
    wide = g_w_up.shape[1] // width
    parts = [first] + [second[..., c * width : (c + 1) * width] for c in range(wide)] + [third]
    ffn = jnp.concatenate(parts, axis=-2).astype(bf16)
    dctx_peer, ffn = lax.optimization_barrier((dctx_peer, ffn))
    ffn_parts = place.plane_stage(ffn)
    g_own, g_peer, g_sums = attend_back(
        side_ref, qkv_own, qkv_peer, tables, ctx_own, ctx_peer, dctx_mine, dctx_peer, lse
    )
    ffn = ((ffn_parts[0] + ffn_parts[1]) + (ffn_parts[2] + ffn_parts[3])).astype(bf16)
    ffn = place.line_stage(ffn)
    n_down = g_w_down.shape[0] // devices
    n_row = width // devices
    r_w_down = ffn[:n_down]
    r_w_up = jnp.concatenate(
        [ffn[n_down + c * n_row : n_down + (c + 1) * n_row] for c in range(wide)], axis=1
    )
    r_w_out = ffn[n_down + wide * n_row :]

    g_part_peer = right_dot(g_peer, w_own).astype(bf16)
    g_part_got = swap(g_part_peer)
    g_w_qkv = left_dot(normed1_own, g_own) + left_dot(normed1_peer, g_peer)
    core_w_qkv = place.core_stage(place.blocks(g_w_qkv.astype(bf16))).astype(bf16)
    g_part_own = right_dot(g_own, w_own)

    bias_sums = jnp.sum(g_sums, axis=0)
    w_wide = w_own.astype(f32)
    g_shift1 = jnp.sum(w_wide * bias_sums, axis=1)
    g_gain1 = (jnp.sum(w_wide * g_w_qkv, axis=1) - shift1 * g_shift1) / gain1
    zero_half = jnp.zeros((hw,), f32)
    g_bias_q = in_order(bias_sums[:hw], zero_half, 0)
    g_bias_v = in_order(bias_sums[2 * hw :], zero_half, 0)
    vectors = (g_gain1, g_shift1, g_bias_q, g_bias_v, g_bias_out, g_gain2, g_shift2, g_bias_down)
    packed = [v.reshape(devices, n_row, 1) for v in vectors]
    packed.append(jnp.swapaxes(g_bias_up.reshape(devices, wide, n_row), 1, 2))
    packed = jnp.concatenate(packed, axis=2)
    columns = packed.shape[2]
    coarse = packed.astype(bf16)
    fine = (packed - coarse.astype(f32)).astype(bf16)
    lanes = jnp.zeros((devices, n_row, 128 - 2 * columns), bf16)
    lanes = jnp.concatenate([coarse, fine, lanes], axis=2).reshape(width, 128)

    core_lanes = place.core_stage(place.blocks(lanes))
    tail_wide = 3 * hw

    def resplit(value):
        sums = value[..., :columns] + value[..., columns : 2 * columns]
        high = sums.astype(bf16)
        low = (sums - high.astype(f32)).astype(bf16)
        return jnp.concatenate([high, low, value[..., 2 * columns :].astype(bf16)], axis=-1)

    tail = jnp.concatenate([core_w_qkv, resplit(core_lanes)], axis=-1)
    kept, across, above, beyond = place.plane_stage(tail)
    mine = (kept + above)[..., :tail_wide]
    theirs = (across + beyond)[..., :tail_wide]
    sums = ((kept + across) + (above + beyond))[..., tail_wide:]
    tail = jnp.concatenate([mine.astype(bf16), theirs.astype(bf16), resplit(sums)], axis=-1)
    tail = place.line_stage(tail)
    r_w_qkv = in_order(
        tail[:, :tail_wide].reshape(n_row, 3, hw), tail[:, tail_wide : 2 * tail_wide].reshape(n_row, 3, hw), 2
    ).reshape(n_row, 3 * width)
    sums = tail[:, 2 * tail_wide : 2 * tail_wide + columns] + tail[:, 2 * tail_wide + columns : 2 * tail_wide + 2 * columns]
    sums = sums.T
    r_gain1, r_shift1, r_bias_q, r_bias_v, r_bias_out, r_gain2, r_shift2, r_bias_down = [sums[k] for k in range(8)]
    r_bias_up = sums[8:].reshape(wide * n_row)

    n1_own, rate1 = norm_parts(inputs)
    g_normed1 = g_part_own + g_part_got.astype(f32)
    grad_x = g_hidden + norm_back(g_normed1, gain1, n1_own, rate1)
    return (
        output.reshape(row_count, half, width),
        grad_x.reshape(row_count, half, width),
        r_gain1,
        r_shift1,
        r_w_qkv,
        r_bias_q,
        r_bias_v,
        r_w_out,
        r_bias_out,
        r_gain2,
        r_shift2,
        r_w_up,
        r_bias_up,
        r_w_down,
        r_bias_down,
    )


def solution(mesh):
    both = P(("rows", "seq"))
    both_wide = P(("rows", "seq"), None)
    tokens = P("rows", "seq", None)

    return jax.shard_map(
        per_device,
        mesh=mesh,
        in_specs=(tokens, tokens) + (P(),) * 13 + (P("rows", None), P("rows", None)),
        out_specs=(
            tokens,
            tokens,
            both,
            both,
            both_wide,
            both,
            both,
            both_wide,
            both,
            both,
            both,
            both_wide,
            both,
            both_wide,
            both,
        ),
        check_vma=False,
    )
```

```python
import functools

import jax
import jax.numpy as jnp
from jax import lax
from jax.experimental import pallas as pl
from jax.experimental.pallas import tpu as pltpu
from jax.sharding import PartitionSpec as P


HEAD_DIM = 64
BQ = 128
BK = 512
PAIR = 2 * HEAD_DIM
LOG2E = 1.4426950408889634
NEG = -1e30

f32 = jnp.float32
bf16 = jnp.bfloat16


def left_dot(left, right):
    return lax.dot_general(left, right, (((0,), (0,)), ((), ())), preferred_element_type=f32)


def right_dot(left, right):
    return lax.dot_general(left, right, (((1,), (1,)), ((), ())), preferred_element_type=f32)


def mm(left, right):
    return jnp.dot(left, right, preferred_element_type=f32)


def stack_heads(block):
    lane = lax.broadcasted_iota(jnp.int32, block.shape, 1)
    zero = jnp.zeros_like(block)
    return jnp.concatenate(
        [jnp.where(lane < HEAD_DIM, block, zero), jnp.where(lane < HEAD_DIM, zero, block)], axis=0
    )


def block_bias(kseg_ref, qseg_ref, qs, ks):
    same = kseg_ref[pl.ds(ks, BK), :] == qseg_ref[0:1, pl.ds(qs, BQ)]
    row = lax.broadcasted_iota(jnp.int32, (BK, BQ), 0)
    col = lax.broadcasted_iota(jnp.int32, (BK, BQ), 1)
    same = same | ((row - col) == (qs - ks))
    bias = jnp.where(same, 0.0, NEG)
    return jnp.concatenate([bias, bias], axis=1)


def gather_halves(dest, own_ref, peer_ref, side):
    half = own_ref.shape[0]
    own_at = side * half
    peer_at = half - own_at
    step = BQ // 2

    def move(i, _):
        at = pl.multiple_of(i * step, step)
        dest[pl.ds(pl.multiple_of(own_at + at, step), step), :] = own_ref[pl.ds(at, step), :]
        dest[pl.ds(pl.multiple_of(peer_at + at, step), step), :] = peer_ref[pl.ds(at, step), :]
        return 0

    lax.fori_loop(0, half // step, move, 0)


def copy_rows(dest_ref, source, start):
    step = BQ // 2

    def move(i, _):
        at = pl.multiple_of(i * step, step)
        dest_ref[pl.ds(at, step), :] = source[pl.ds(pl.multiple_of(start + at, step), step), :]
        return 0

    lax.fori_loop(0, dest_ref.shape[0] // step, move, 0)


def transpose_columns(dest, source, full, first, pairs):
    dest[:, full:] = jnp.zeros((dest.shape[0], dest.shape[1] - full), dest.dtype)

    def move(i, _):
        at = pl.multiple_of(i * BQ, BQ)
        for p in range(pairs):
            dest[p * PAIR : (p + 1) * PAIR, pl.ds(at, BQ)] = source[
                pl.ds(at, BQ), first + p * PAIR : first + (p + 1) * PAIR
            ].T
        return 0

    lax.fori_loop(0, full // BQ, move, 0)


def forward_kernel(second, side_ref, start_ref, count_ref, own_ref, peer_ref, kseg_ref, qseg_ref, *rest):
    if second:
        edge_in, lse_in, ctx_ref, lse_ref, qkv, ctx, vt, qst, acc = rest
    else:
        ctx_ref, edge_ref, lse_ref, qkv, ctx, vt, qst, acc = rest
    half, cols = own_ref.shape
    full = 2 * half
    width = cols // 3
    pairs = width // PAIR
    mid = half // BQ
    side = side_ref[0]
    gather_halves(qkv, own_ref, peer_ref, side)
    qkv[full:, :] = jnp.zeros((qkv.shape[0] - full, cols), bf16)
    transpose_columns(vt, qkv, full, 2 * width, pairs)
    edge_at = pl.multiple_of(mid * BQ + side * (BQ // 2), BQ // 2)
    if second:
        first_block = side * (mid + 1)
        last_block = first_block + mid
        lse_ref[...] = lse_in[...]
        ctx[pl.ds(edge_at, BQ // 2), :] = edge_in[...]
    else:
        first_block = (1 - side) * mid
        last_block = first_block + mid + 1
        lse_ref[...] = jnp.zeros(lse_ref.shape, f32)

    def q_step(i, _):
        qs = pl.multiple_of(i * BQ, BQ)
        start = start_ref[i]
        for p in range(pairs):
            blk = qkv[pl.ds(qs, BQ), p * PAIR : (p + 1) * PAIR]
            qst[p] = stack_heads(blk * jnp.asarray(HEAD_DIM**-0.5, bf16))
            acc[p] = jnp.zeros((PAIR, BQ), f32)

        def k_step(t, carry):
            ks = pl.multiple_of(start + t * BK, BQ)
            bias = block_bias(kseg_ref, qseg_ref, qs, ks)
            new = []
            for p in range(pairs):
                top, total = carry[p]
                s = right_dot(qkv[pl.ds(ks, BK), width + p * PAIR : width + (p + 1) * PAIR], qst[p])
                s = s * LOG2E + bias
                top_new = jnp.maximum(top, jnp.max(s, axis=0, keepdims=True))
                e = jnp.exp2(s - top_new)
                alpha = jnp.exp2(top - top_new)
                total = total * alpha + jnp.sum(e, axis=0, keepdims=True)
                e = e.astype(bf16)
                for h in range(2):
                    rows = slice(h * HEAD_DIM, (h + 1) * HEAD_DIM)
                    lanes = slice(h * BQ, (h + 1) * BQ)
                    part = mm(vt[p * PAIR + h * HEAD_DIM : p * PAIR + (h + 1) * HEAD_DIM, pl.ds(ks, BK)], e[:, lanes])
                    acc[p, rows, :] = acc[p, rows, :] * alpha[:, lanes] + part
                new.append((top_new, total))
            return tuple(new)

        init = tuple((jnp.full((1, 2 * BQ), NEG, f32), jnp.zeros((1, 2 * BQ), f32)) for _ in range(pairs))
        done = lax.fori_loop(0, count_ref[i], k_step, init)
        for p in range(pairs):
            top, total = done[p]
            inv = 1.0 / total
            parts = []
            for h in range(2):
                parts.append(acc[p, h * HEAD_DIM : (h + 1) * HEAD_DIM, :] * inv[:, h * BQ : (h + 1) * BQ])
            ctx[pl.ds(qs, BQ), p * PAIR : (p + 1) * PAIR] = jnp.concatenate(parts, axis=0).T.astype(bf16)
            lse_ref[p, pl.ds(i, 1), :] = top + jnp.log2(total)
        return 0

    lax.fori_loop(first_block, last_block, q_step, 0)
    if second:
        copy_rows(ctx_ref, ctx, side * half)
    else:
        copy_rows(ctx_ref, ctx, (1 - side) * half)
        edge_ref[...] = ctx[pl.ds(edge_at, BQ // 2), :]


def backward_kernel(
    side_ref,
    start_ref,
    count_ref,
    own_ref,
    peer_ref,
    kseg_ref,
    qseg_ref,
    ctx_own_ref,
    ctx_peer_ref,
    dctx_own_ref,
    dctx_peer_ref,
    lse_ref,
    out_own_ref,
    out_peer_ref,
    sums_ref,
    qkv,
    ctx,
    dctx,
    out,
    kt,
    qst,
    dst,
    acc,
    dk,
    dv,
):
    half, cols = own_ref.shape
    full = 2 * half
    width = cols // 3
    pairs = width // PAIR
    side = side_ref[0]
    gather_halves(qkv, own_ref, peer_ref, side)
    gather_halves(ctx, ctx_own_ref, ctx_peer_ref, side)
    gather_halves(dctx, dctx_own_ref, dctx_peer_ref, side)
    qkv[full:, :] = jnp.zeros((qkv.shape[0] - full, cols), bf16)
    transpose_columns(kt, qkv, full, width, pairs)

    def clear(i, _):
        at = pl.multiple_of(i * BQ, BQ)
        dk[pl.ds(at, BQ), :] = jnp.zeros((BQ, width), f32)
        dv[pl.ds(at, BQ), :] = jnp.zeros((BQ, width), f32)
        return 0

    lax.fori_loop(0, dk.shape[0] // BQ, clear, 0)
    head_row = lax.broadcasted_iota(jnp.int32, (8, PAIR), 0)
    head_lane = lax.broadcasted_iota(jnp.int32, (8, PAIR), 1) // HEAD_DIM
    pick = (head_row == head_lane).astype(f32)

    def q_step(i, _):
        qs = pl.multiple_of(i * BQ, BQ)
        start = start_ref[i]
        stats = []
        for p in range(pairs):
            lanes = slice(p * PAIR, (p + 1) * PAIR)
            blk = qkv[pl.ds(qs, BQ), lanes]
            qst[p] = stack_heads(blk * jnp.asarray(HEAD_DIM**-0.5, bf16))
            grad = dctx[pl.ds(qs, BQ), lanes]
            dst[p] = stack_heads(grad)
            acc[p] = jnp.zeros((PAIR, BQ), f32)
            prod = grad.astype(f32) * ctx[pl.ds(qs, BQ), lanes].astype(f32)
            dots = lax.dot_general(
                pick, prod, (((1,), (1,)), ((), ())), precision=lax.Precision.HIGHEST, preferred_element_type=f32
            )
            stats.append((lse_ref[p, pl.ds(i, 1), :], jnp.concatenate([dots[0:1], dots[1:2]], axis=1)))

        def k_step(t, _):
            ks = pl.multiple_of(start + t * BK, BQ)
            bias = block_bias(kseg_ref, qseg_ref, qs, ks)
            for p in range(pairs):
                lanes = slice(p * PAIR, (p + 1) * PAIR)
                lse, dots = stats[p]
                s = right_dot(qkv[pl.ds(ks, BK), width + p * PAIR : width + (p + 1) * PAIR], qst[p])
                e = jnp.exp2(s * LOG2E + bias - lse)
                dp = right_dot(qkv[pl.ds(ks, BK), 2 * width + p * PAIR : 2 * width + (p + 1) * PAIR], dst[p])
                ds = (e * (dp - dots)).astype(bf16)
                dv[pl.ds(ks, BK), lanes] += mm(e.astype(bf16), dst[p])
                dk[pl.ds(ks, BK), lanes] += mm(ds, qst[p])
                whole = mm(kt[p * PAIR : (p + 1) * PAIR, pl.ds(ks, BK)], ds)
                for h in range(2):
                    rows = slice(h * HEAD_DIM, (h + 1) * HEAD_DIM)
                    acc[p, rows, :] = acc[p, rows, :] + whole[rows, h * BQ : (h + 1) * BQ]
            return 0

        lax.fori_loop(0, count_ref[i], k_step, 0)
        for p in range(pairs):
            out[pl.ds(qs, BQ), p * PAIR : (p + 1) * PAIR] = (acc[p] * HEAD_DIM**-0.5).T.astype(bf16)
        return 0

    lax.fori_loop(0, full // BQ, q_step, 0)

    def finish(i, sums):
        at = pl.multiple_of(i * BQ, BQ)
        out[pl.ds(at, BQ), width : 2 * width] = dk[pl.ds(at, BQ), :].astype(bf16)
        out[pl.ds(at, BQ), 2 * width :] = dv[pl.ds(at, BQ), :].astype(bf16)
        block = out[pl.ds(at, BQ), :].astype(f32).reshape(BQ // 8, 8, cols)
        return sums + jnp.sum(block, axis=0)

    sums_ref[...] = lax.fori_loop(0, full // BQ, finish, jnp.zeros((8, cols), f32))
    copy_rows(out_own_ref, out, side * half)
    copy_rows(out_peer_ref, out, (1 - side) * half)


def project_kernel(x_ref, gain_ref, shift_ref, w_ref, bias_ref, normed_ref, qkv_ref):
    n, _ = norm_parts(x_ref[...].astype(f32))
    normed = (n * gain_ref[...] + shift_ref[...]).astype(bf16)
    normed_ref[...] = normed
    qkv_ref[...] = (mm(normed, w_ref[...]) + bias_ref[...]).astype(bf16)


def project(x, gain, shift, w, bias):
    half, width = x.shape
    cols = w.shape[1]
    step = half // 4
    fixed = lambda i: (0, 0)
    moving = lambda i: (i, 0)
    return pl.pallas_call(
        project_kernel,
        grid=(4,),
        out_shape=(jax.ShapeDtypeStruct((half, width), bf16), jax.ShapeDtypeStruct((half, cols), bf16)),
        in_specs=[
            pl.BlockSpec((step, width), moving),
            pl.BlockSpec((1, width), fixed),
            pl.BlockSpec((1, width), fixed),
            pl.BlockSpec((width, cols), fixed),
            pl.BlockSpec((1, cols), fixed),
        ],
        out_specs=(pl.BlockSpec((step, width), moving), pl.BlockSpec((step, cols), moving)),
    )(x, gain[None], shift[None], w, bias[None])


def smem():
    return pl.BlockSpec(memory_space=pltpu.SMEM)


def vmem():
    return pl.BlockSpec(memory_space=pltpu.VMEM)


def attend(side, qkv_own, qkv_peer, tables, earlier=None):
    half, cols = qkv_own.shape
    full = 2 * half
    width = cols // 3
    pairs = width // PAIR
    padded = full + BK - BQ
    starts, counts, kseg, qseg = tables
    ctx_shape = jax.ShapeDtypeStruct((half, width), bf16)
    edge_shape = jax.ShapeDtypeStruct((BQ // 2, width), bf16)
    lse_shape = jax.ShapeDtypeStruct((pairs, full // BQ, 2 * BQ), f32)
    second = earlier is not None
    return pl.pallas_call(
        functools.partial(forward_kernel, second),
        out_shape=(ctx_shape, lse_shape) if second else (ctx_shape, edge_shape, lse_shape),
        in_specs=[smem()] * 3 + [vmem()] * (6 if second else 4),
        out_specs=(vmem(),) * (2 if second else 3),
        scratch_shapes=[
            pltpu.VMEM((padded, cols), bf16),
            pltpu.VMEM((full, width), bf16),
            pltpu.VMEM((width, padded), bf16),
            pltpu.VMEM((pairs, 2 * BQ, PAIR), bf16),
            pltpu.VMEM((pairs, PAIR, BQ), f32),
        ],
        name="attn_own" if second else "attn_peer",
    )(side, starts, counts, qkv_own, qkv_peer, kseg, qseg, *(earlier or ()))


def attend_back(side, qkv_own, qkv_peer, tables, ctx_own, ctx_peer, dctx_own, dctx_peer, lse):
    half, cols = qkv_own.shape
    full = 2 * half
    width = cols // 3
    pairs = width // PAIR
    padded = full + BK - BQ
    starts, counts, kseg, qseg = tables
    return pl.pallas_call(
        backward_kernel,
        out_shape=(
            jax.ShapeDtypeStruct((half, cols), bf16),
            jax.ShapeDtypeStruct((half, cols), bf16),
            jax.ShapeDtypeStruct((8, cols), f32),
        ),
        in_specs=[smem()] * 3 + [vmem()] * 9,
        out_specs=(vmem(),) * 3,
        scratch_shapes=[
            pltpu.VMEM((padded, cols), bf16),
            pltpu.VMEM((full, width), bf16),
            pltpu.VMEM((full, width), bf16),
            pltpu.VMEM((full, cols), bf16),
            pltpu.VMEM((width, padded), bf16),
            pltpu.VMEM((pairs, 2 * BQ, PAIR), bf16),
            pltpu.VMEM((pairs, 2 * BQ, PAIR), bf16),
            pltpu.VMEM((pairs, PAIR, BQ), f32),
            pltpu.VMEM((padded, width), f32),
            pltpu.VMEM((padded, width), f32),
        ],
        name="attn_bwd",
    )(side, starts, counts, qkv_own, qkv_peer, kseg, qseg, ctx_own, ctx_peer, dctx_own, dctx_peer, lse)


def attention_tables(seg, valid):
    full = seg.shape[0]
    first = seg[::BQ]
    last = seg[BQ - 1 :: BQ]
    lo = jnp.sum((seg[None, :] < first[:, None]).astype(jnp.int32), axis=1)
    hi = jnp.sum((seg[None, :] <= last[:, None]).astype(jnp.int32), axis=1)
    starts = (lo // BQ) * BQ
    counts = (hi - starts + BK - 1) // BK
    keys = jnp.where(valid == 1, seg, -1)
    keys = jnp.concatenate([keys, jnp.full((BK - BQ,), -1, jnp.int32)])
    kseg = jnp.broadcast_to(keys[:, None], (full + BK - BQ, BQ))
    qseg = jnp.broadcast_to(seg[None, :], (8, full))
    return starts, counts, kseg, qseg


def norm_parts(values):
    center = jnp.mean(values, axis=-1, keepdims=True)
    centered = values - center
    spread = jnp.mean(centered * centered, axis=-1, keepdims=True)
    rate = lax.rsqrt(spread + 1e-06)
    return centered * rate, rate


def norm_back(grad, gain, n, rate):
    e = grad * gain
    return rate * (e - jnp.mean(e, axis=-1, keepdims=True) - n * jnp.mean(e * n, axis=-1, keepdims=True))


def swap(value):
    return lax.ppermute(value, "seq", [(0, 1), (1, 0)])


def take(value, index, axis):
    return lax.dynamic_index_in_dim(value, index, axis=axis, keepdims=False)


class Place:
    def __init__(self):
        self.rows = lax.axis_size("rows")
        self.lines = self.rows // 4
        r = lax.axis_index("rows")
        self.side = lax.axis_index("seq")
        self.core = r % 2
        self.high = (r // 2) % 2
        self.line = r // 4

    def send(self, value, row_flip, side_flip):
        pairs = [
            (2 * r + s, 2 * (r ^ row_flip) + (s ^ side_flip)) for r in range(self.rows) for s in range(2)
        ]
        return lax.ppermute(value, ("rows", "seq"), pairs)

    def blocks(self, value):
        devices = 2 * self.rows
        return value.reshape((self.lines, 2, 2, 2, value.shape[0] // devices) + value.shape[1:])

    def core_stage(self, value):
        other = self.send(take(value, 1 - self.core, 2), 1, 0)
        return take(value, self.core, 2).astype(f32) + other.astype(f32)

    def plane_stage(self, value):
        got = [take(take(value, self.side, 2), self.high, 1)]
        for high, side in ((0, 1), (1, 0), (1, 1)):
            part = take(take(value, self.side ^ side, 2), self.high ^ high, 1)
            got.append(self.send(part, 2 * high, side))
        return [g.astype(f32) for g in got]

    def line_stage(self, value):
        total = take(value, self.line, 0).astype(f32)
        for step in range(1, self.lines):
            total = total + self.send(take(value, self.line ^ step, 0), 4 * step, 0).astype(f32)
        return total


def per_device(
    layer_input,
    out_cotangent,
    gain1,
    shift1,
    w_qkv,
    bias_q,
    bias_v,
    w_out,
    bias_out,
    gain2,
    shift2,
    w_up,
    bias_up,
    w_down,
    bias_down,
    segment_ids,
    valid_mask,
):
    row_count, half, width = layer_input.shape
    full = 2 * half
    hw = width // 2
    side = lax.axis_index("seq")
    devices = lax.axis_size("rows") * 2
    is_low = side == 0

    def in_order(mine, other, axis):
        return jnp.where(
            is_low, jnp.concatenate([mine, other], axis=axis), jnp.concatenate([other, mine], axis=axis)
        )

    def side_columns(value, low):
        parts = []
        for at in range(0, value.shape[-1], width):
            parts.append(jnp.where(low, value[..., at : at + hw], value[..., at + hw : at + width]))
        return jnp.concatenate(parts, axis=-1)

    x_own = layer_input.reshape(half, width)
    x_peer = swap(x_own)
    tables = attention_tables(segment_ids.reshape(full), valid_mask.reshape(full))
    w_own = side_columns(w_qkv, is_low)
    bias_own = side_columns(jnp.concatenate([bias_q, jnp.zeros_like(bias_q), bias_v]), is_low)
    side_ref = side.reshape(1).astype(jnp.int32)

    normed1_own, qkv_own = project(x_own, gain1, shift1, w_own, bias_own)
    normed1_peer, qkv_peer = project(x_peer, gain1, shift1, w_own, bias_own)
    ctx_peer, ctx_edge, lse = attend(side_ref, qkv_own, qkv_peer, tables)
    ctx_got = swap(ctx_peer)
    ctx_own, lse = attend(side_ref, qkv_own, qkv_peer, tables, (ctx_edge, lse))

    context = in_order(ctx_own, ctx_got, 1)
    inputs = x_own.astype(f32)
    hidden = inputs + mm(context, w_out) + bias_out
    n2, rate2 = norm_parts(hidden)
    normed2 = (n2 * gain2 + shift2).astype(bf16)
    upper = mm(normed2, w_up) + bias_up
    cdf = 0.5 * (1.0 + lax.erf(upper * (0.5**0.5)))
    act = (upper * cdf).astype(bf16)
    output = hidden + mm(act, w_down) + bias_down

    g_ffn = out_cotangent.reshape(half, width)
    g_wide = g_ffn.astype(f32)
    g_bias_down = jnp.sum(g_wide, axis=0)
    slope = cdf + upper * jnp.exp(-0.5 * upper * upper) * 0.3989422804014327
    g_upper = (right_dot(g_ffn, w_down) * slope).astype(bf16)
    g_normed2 = right_dot(g_upper, w_up)
    g_gain2 = jnp.sum(g_normed2 * n2, axis=0)
    g_shift2 = jnp.sum(g_normed2, axis=0)
    g_hidden = g_wide + norm_back(g_normed2, gain2, n2, rate2)
    g_attn = g_hidden.astype(bf16)

    w_out_mine = jnp.where(is_low, w_out[:hw], w_out[hw:])
    w_out_peer = jnp.where(is_low, w_out[hw:], w_out[:hw])
    dctx_part = right_dot(g_attn, w_out_peer).astype(bf16)
    dctx_peer = swap(dctx_part)
    dctx_mine = right_dot(g_attn, w_out_mine).astype(bf16)

    g_w_down = left_dot(act, g_ffn).astype(bf16)
    g_w_up = left_dot(normed2, g_upper).astype(bf16)
    g_w_out = left_dot(context, g_attn).astype(bf16)
    g_bias_up = jnp.sum(g_upper.astype(f32), axis=0)
    g_bias_out = jnp.sum(g_attn.astype(f32), axis=0)

    place = Place()
    first = place.core_stage(place.blocks(g_w_down))
    second = place.core_stage(place.blocks(g_w_up))
    third = place.core_stage(place.blocks(g_w_out))
    wide = g_w_up.shape[1] // width
    parts = [first] + [second[..., c * width : (c + 1) * width] for c in range(wide)] + [third]
    ffn = jnp.concatenate(parts, axis=-2).astype(bf16)
    dctx_peer, ffn = lax.optimization_barrier((dctx_peer, ffn))
    ffn_parts = place.plane_stage(ffn)
    g_own, g_peer, g_sums = attend_back(
        side_ref, qkv_own, qkv_peer, tables, ctx_own, ctx_peer, dctx_mine, dctx_peer, lse
    )
    ffn = ((ffn_parts[0] + ffn_parts[1]) + (ffn_parts[2] + ffn_parts[3])).astype(bf16)
    ffn = place.line_stage(ffn)
    n_down = g_w_down.shape[0] // devices
    n_row = width // devices
    r_w_down = ffn[:n_down]
    r_w_up = jnp.concatenate(
        [ffn[n_down + c * n_row : n_down + (c + 1) * n_row] for c in range(wide)], axis=1
    )
    r_w_out = ffn[n_down + wide * n_row :]

    g_part_peer = right_dot(g_peer, w_own).astype(bf16)
    g_part_got = swap(g_part_peer)
    g_w_qkv = left_dot(normed1_own, g_own) + left_dot(normed1_peer, g_peer)
    core_w_qkv = place.core_stage(place.blocks(g_w_qkv.astype(bf16))).astype(bf16)
    g_part_own = right_dot(g_own, w_own)

    bias_sums = jnp.sum(g_sums, axis=0)
    w_wide = w_own.astype(f32)
    g_shift1 = jnp.sum(w_wide * bias_sums, axis=1)
    g_gain1 = (jnp.sum(w_wide * g_w_qkv, axis=1) - shift1 * g_shift1) / gain1
    zero_half = jnp.zeros((hw,), f32)
    g_bias_q = in_order(bias_sums[:hw], zero_half, 0)
    g_bias_v = in_order(bias_sums[2 * hw :], zero_half, 0)
    vectors = (g_gain1, g_shift1, g_bias_q, g_bias_v, g_bias_out, g_gain2, g_shift2, g_bias_down)
    packed = [v.reshape(devices, n_row, 1) for v in vectors]
    packed.append(jnp.swapaxes(g_bias_up.reshape(devices, wide, n_row), 1, 2))
    packed = jnp.concatenate(packed, axis=2)
    columns = packed.shape[2]
    coarse = packed.astype(bf16)
    fine = (packed - coarse.astype(f32)).astype(bf16)
    lanes = jnp.zeros((devices, n_row, 128 - 2 * columns), bf16)
    lanes = jnp.concatenate([coarse, fine, lanes], axis=2).reshape(width, 128)

    core_lanes = place.core_stage(place.blocks(lanes))
    tail_wide = 3 * hw

    def resplit(value):
        sums = value[..., :columns] + value[..., columns : 2 * columns]
        high = sums.astype(bf16)
        low = (sums - high.astype(f32)).astype(bf16)
        return jnp.concatenate([high, low, value[..., 2 * columns :].astype(bf16)], axis=-1)

    tail = jnp.concatenate([core_w_qkv, resplit(core_lanes)], axis=-1)
    kept, across, above, beyond = place.plane_stage(tail)
    mine = (kept + above)[..., :tail_wide]
    theirs = (across + beyond)[..., :tail_wide]
    sums = ((kept + across) + (above + beyond))[..., tail_wide:]
    tail = jnp.concatenate([mine.astype(bf16), theirs.astype(bf16), resplit(sums)], axis=-1)
    tail = place.line_stage(tail)
    r_w_qkv = in_order(
        tail[:, :tail_wide].reshape(n_row, 3, hw), tail[:, tail_wide : 2 * tail_wide].reshape(n_row, 3, hw), 2
    ).reshape(n_row, 3 * width)
    sums = tail[:, 2 * tail_wide : 2 * tail_wide + columns] + tail[:, 2 * tail_wide + columns : 2 * tail_wide + 2 * columns]
    sums = sums.T
    r_gain1, r_shift1, r_bias_q, r_bias_v, r_bias_out, r_gain2, r_shift2, r_bias_down = [sums[k] for k in range(8)]
    r_bias_up = sums[8:].reshape(wide * n_row)

    n1_own, rate1 = norm_parts(inputs)
    g_normed1 = g_part_own + g_part_got.astype(f32)
    grad_x = g_hidden + norm_back(g_normed1, gain1, n1_own, rate1)
    return (
        output.reshape(row_count, half, width),
        grad_x.reshape(row_count, half, width),
        r_gain1,
        r_shift1,
        r_w_qkv,
        r_bias_q,
        r_bias_v,
        r_w_out,
        r_bias_out,
        r_gain2,
        r_shift2,
        r_w_up,
        r_bias_up,
        r_w_down,
        r_bias_down,
    )


def solution(mesh):
    both = P(("rows", "seq"))
    both_wide = P(("rows", "seq"), None)
    tokens = P("rows", "seq", None)

    return jax.shard_map(
        per_device,
        mesh=mesh,
        in_specs=(tokens, tokens) + (P(),) * 13 + (P("rows", None), P("rows", None)),
        out_specs=(
            tokens,
            tokens,
            both,
            both,
            both_wide,
            both,
            both,
            both_wide,
            both,
            both,
            both,
            both_wide,
            both,
            both_wide,
            both,
        ),
        check_vma=False,
    )
```
